32 devices in a mesh: slides: 2 (over y), tiles: 4 (over z), heads: 4 (over x, core).
Axes of the slice: x: 2, y: 2, z: 4, core: 2. Of those that a mesh axis runs over, the one named last changes fastest.
Arguments:
- pixels: bfloat16 [32, 4096, 192], P(('slides', 'tiles', 'heads')), parts along dimension 0, may hold values from -6 to 6
- w_stem: bfloat16 [192, 64], replicated, may hold values from -0.4375 to 0.4375
- w_conv1: bfloat16 [4, 9, 16, 32], replicated, may hold values from -0.5 to 0.5
- w_conv2: bfloat16 [4, 9, 32, 64], replicated, may hold values from -0.375 to 0.375
- w_key: bfloat16 [256, 512], P(None, 'heads'), may hold values from -0.375 to 0.375
- w_value: bfloat16 [256, 512], P(None, 'heads'), may hold values from -0.375 to 0.375
- queries: bfloat16 [512, 512], P(None, 'heads'), may hold values from -104 to 104
- tile_count: int32 [32], P(('slides', 'tiles', 'heads')), parts along dimension 0, may hold values from 0 to 1, as said below
- tissue: int32 [32], P(('slides', 'tiles', 'heads')), parts along dimension 0, may hold values from 17 to 256, as said below
- adjacency: int32 [32, 3], P(('slides', 'tiles', 'heads')), parts along dimension 0, may hold values from -1 to 0, as said below
Outputs:
- pooled: bfloat16 [1024, 512], P(('slides', 'tiles'), 'heads'), parts along dimension 0
The draws below stay inside these ranges and needn't reach their ends.
There are 2 independent parts, one for each index of `slides`. The reference program is written for one: setup_inputs(seed, part) draws one part's arguments, and reference() takes and returns one part's arrays. A program takes and returns all parts, laid end to end along the dimension named above; an argument that names none is the same for every part. Nothing has to cross between parts.
Inputs may be any that keep to these rules, and one draw needn't show every extreme that they name: Device g (order of tiles+heads) holds tiles in its slots 0 to tile_count[g] - 1; the first device holds 1, the second 1; other devices may hold none. Tokens 0 to tissue[s] - 1 of slot s, raster order, are tissue; slot 0 is all tissue. `adjacency`: A code below 1 names a slot of the previous device along tiles+heads, a code c of 1 or more names slot c - 1 of the same device, earlier than the slot itself; -1 is background.
All inputs are finite; a program needn't handle non-finite values.
Results may differ from the reference program's by a relative error of at most 0.012.
The reference program's roundings to bfloat16 on the way count: a program that leaves them out, or rounds other values in their place, can miss the bound.
Values may be sent and summed in bfloat16 or wider, within the bound.
No kernel may reach another device: no remote copies, remote signals or barrier semaphores. Data moves between devices by JAX's collectives and lax.ppermute only.
A program may use at most 128 MiB of HBM per device.

```python
import jax
import jax.numpy as jnp
from jax import lax

STEM_GRID = 64
PATCH_DIM = 192
C_STEM = 64
C_MID = 128
C_OUT = 256
GROUPS = 4
HEADS = 8
HEAD_DIM = 64
LATENTS = 512
SLOTS = 1
TOK_TILE = 256
DL = 512
GROUPS_T = 16
SLOT_ALL = 16


def draw_queries(key, part):
    return jnp.clip(3.0 * jax.random.normal(key, (LATENTS, DL), jnp.float32), -12.0, 12.0).astype(jnp.bfloat16)


def draw_tile_count(key, part):
    counts = jax.random.randint(key, (GROUPS_T,), 0, SLOTS + 1)
    counts = counts.at[0].set(SLOTS)
    return counts.at[1].set(1).astype(jnp.int32)


def draw_tissue(key, part):
    counts = jax.random.randint(key, (SLOT_ALL,), TOK_TILE // 16 + 1, TOK_TILE + 1)
    counts = counts.at[0].set(TOK_TILE)
    return counts.at[1].set(TOK_TILE // 16 + 1).astype(jnp.int32)


def draw_adjacency(key, part):
    slot_pos = jnp.arange(SLOT_ALL, dtype=jnp.int32) % SLOTS
    reach = SLOTS + slot_pos + 1
    raw_bits = jax.random.randint(key, (SLOT_ALL, 3), 0, 1 << 20)
    above = raw_bits[:, 0] % reach - 1
    diagonal = raw_bits[:, 2] % reach - 1
    beside = jnp.where(raw_bits[:, 1] % 4 == 0, -1, SLOTS + slot_pos - 1)
    beside = beside.at[SLOTS - 1].set(2 * SLOTS - 2)
    return jnp.stack([above, beside, diagonal], axis=1).astype(jnp.int32)


def block_levels(own_key, dims, shards, least, high):
    def one(position, parts):
        heights = jax.random.uniform(jax.random.fold_in(jax.random.fold_in(own_key, 6), position), (parts,), jnp.float32, least / len(shards), high / len(shards))
        return jnp.repeat(jnp.exp(heights), dims[position] // parts).reshape((-1,) + (1,) * (len(dims) - position - 1))

    gain = one(*shards[0])
    for cut in shards[1:]:
        gain = gain * one(*cut)
    return gain


def normal_values(own_key, extent, deviation, most, pieces=(), held_as=jnp.bfloat16):
    values = deviation * jax.random.normal(own_key, extent, jnp.float32)
    if pieces:
        values = values * block_levels(own_key, extent, pieces, -0.22, 0.18)
    return jnp.clip(values, -most, most).astype(held_as)


def setup_inputs(seed: int = 0, part: int = 0) -> dict:
    keys = jax.random.split(jax.random.key(seed), 11)
    part_keys = jax.random.split(jax.random.fold_in(keys[10], part), 11)
    return {
        "pixels": normal_values(part_keys[0], (SLOT_ALL, STEM_GRID * STEM_GRID, PATCH_DIM), 1.0, 6.0, ((0, 16),)),
        "w_stem": normal_values(keys[1], (PATCH_DIM, C_STEM), PATCH_DIM ** -0.5, 0.4375),
        "w_conv1": normal_values(keys[2], (GROUPS, 9, C_STEM // GROUPS, C_MID // GROUPS), (9 * C_STEM // GROUPS) ** -0.5, 0.5),
        "w_conv2": normal_values(keys[3], (GROUPS, 9, C_MID // GROUPS, C_OUT // GROUPS), (9 * C_MID // GROUPS) ** -0.5, 0.375),
        "w_key": normal_values(keys[4], (C_OUT, DL), C_OUT ** -0.5, 0.375, ((1, 4),)),
        "w_value": normal_values(keys[5], (C_OUT, DL), C_OUT ** -0.5, 0.375, ((1, 4),)),
        "queries": draw_queries(jax.random.fold_in(keys[10], 71), part),
        "tile_count": draw_tile_count(jax.random.fold_in(jax.random.fold_in(keys[10], part), 71), part),
        "tissue": draw_tissue(jax.random.fold_in(jax.random.fold_in(keys[10], part), 71), part),
        "adjacency": draw_adjacency(jax.random.fold_in(jax.random.fold_in(keys[10], part), 71), part),
    }


NEG_BIG = -1e+30
LN_EPS = 1e-05

def border_lines(feature_map):
    slot_n = feature_map.shape[0]
    side = feature_map.shape[1]
    channels = feature_map.shape[3]
    return jnp.stack([feature_map[:, side - 1], feature_map[:, :, side - 1]], axis=1).reshape(slot_n, 2, side * channels)

def bordered(inner, earlier, own_lines, adjacency):
    slot_n = inner.shape[0]
    side = inner.shape[1]
    channels = inner.shape[3]
    lines = jnp.concatenate([earlier, own_lines], axis=0)
    source_n = lines.shape[0]
    chooser = (adjacency[:, :, None] == jnp.arange(source_n, dtype=jnp.int32)[None, None, :]).astype(jnp.bfloat16)
    above = jnp.dot(chooser[:, 0], lines[:, 0], preferred_element_type=jnp.float32).astype(jnp.bfloat16).reshape(slot_n, side, channels)
    beside = jnp.dot(chooser[:, 1], lines[:, 1], preferred_element_type=jnp.float32).astype(jnp.bfloat16).reshape(slot_n, side, channels)
    last_pixel = lines[:, 0].reshape(source_n, side, channels)[:, side - 1]
    corner = jnp.dot(chooser[:, 2], last_pixel, preferred_element_type=jnp.float32).astype(jnp.bfloat16)
    first_line = jnp.concatenate([corner[:, None], above], axis=1)
    lower = jnp.concatenate([beside[:, :, None], inner], axis=2)
    return jnp.concatenate([first_line[:, None], lower], axis=1)

def grouped_conv(padded, weight):
    slot_n = padded.shape[0]
    out_side = (padded.shape[1] - 1) // 2
    groups_n = weight.shape[0]
    in_group = weight.shape[2]
    out_group = weight.shape[3]
    windows = jnp.stack([padded[:, tap_row:tap_row + 2 * out_side:2, tap_col:tap_col + 2 * out_side:2, :] for tap_row in range(3) for tap_col in range(3)], axis=3)
    windows = windows.reshape(slot_n, out_side, out_side, 9, groups_n, in_group).astype(jnp.float32)
    summed = jnp.einsum('syxkgc,gkcd->syxgd', windows, weight.astype(jnp.float32), precision=lax.Precision.HIGHEST)
    return summed.reshape(slot_n, out_side, out_side, groups_n * out_group)

def reference(pixels, w_stem, w_conv1, w_conv2, w_key, w_value, queries, tile_count, tissue, adjacency):
    group_n = tile_count.shape[0]

    def encode_step(running, inputs):
        stem_prior, middle_prior = running
        pixel_block, adjacency_block, count_block, tissue_block = inputs
        slot_live = (jnp.arange(SLOTS, dtype=jnp.int32) < count_block).astype(jnp.float32)
        stem_flat = jnp.dot(pixel_block.reshape(SLOTS * STEM_GRID * STEM_GRID, PATCH_DIM), w_stem, preferred_element_type=jnp.float32)
        stem_map = (jnp.maximum(stem_flat, 0.0).reshape(SLOTS, STEM_GRID, STEM_GRID, C_STEM) * slot_live[:, None, None, None]).astype(jnp.bfloat16)
        stem_map = lax.optimization_barrier(stem_map)
        stem_lines = border_lines(stem_map)
        middle = grouped_conv(bordered(stem_map, stem_prior, stem_lines, adjacency_block), w_conv1)
        middle = (jnp.maximum(middle, 0.0) * slot_live[:, None, None, None]).astype(jnp.bfloat16)
        middle = lax.optimization_barrier(middle)
        middle_lines = border_lines(middle)
        deepest = jnp.maximum(grouped_conv(bordered(middle, middle_prior, middle_lines, adjacency_block), w_conv2), 0.0)
        deepest = deepest.reshape(SLOTS * TOK_TILE, C_OUT)
        centred = deepest - lax.optimization_barrier(jnp.mean(deepest, axis=1, keepdims=True))
        normed = (centred * lax.rsqrt(lax.optimization_barrier(jnp.mean(centred * centred, axis=1, keepdims=True)) + LN_EPS)).astype(jnp.bfloat16)
        in_tile = (jnp.arange(TOK_TILE, dtype=jnp.int32)[None, :] < tissue_block[:, None]).astype(jnp.float32)
        valid = (in_tile * slot_live[:, None]).reshape(SLOTS * TOK_TILE)
        return ((stem_lines, middle_lines), (normed, valid))
    start_lines = (jnp.zeros((SLOTS, 2, STEM_GRID * C_STEM), jnp.bfloat16), jnp.zeros((SLOTS, 2, STEM_GRID // 2 * C_MID), jnp.bfloat16))
    inputs = (pixels.reshape(group_n, SLOTS, STEM_GRID * STEM_GRID, PATCH_DIM), adjacency.reshape(group_n, SLOTS, 3), tile_count, tissue.reshape(group_n, SLOTS))
    normed_all, valid_all = lax.scan(encode_step, start_lines, inputs)[1]
    weight_both = jnp.concatenate([w_key, w_value], axis=1)
    query_heads = queries.reshape(LATENTS, HEADS, HEAD_DIM).astype(jnp.float32)
    score_scale = float(HEAD_DIM) ** (-0.5)

    def block_scores(normed_block, valid_block):
        projected = jnp.dot(normed_block, weight_both, preferred_element_type=jnp.float32).astype(jnp.bfloat16)
        projected = lax.optimization_barrier(projected).astype(jnp.float32)
        key_rows = projected[:, :DL].reshape(-1, HEADS, HEAD_DIM)
        value_rows = projected[:, DL:].reshape(-1, HEADS, HEAD_DIM)
        scores = jnp.einsum('lhd,thd->hlt', query_heads, key_rows, precision=lax.Precision.HIGHEST) * score_scale
        scores = jnp.where(valid_block[None, None, :] > 0.5, scores, NEG_BIG)
        return (scores, value_rows)

    def peak_step(running, inputs):
        scores = block_scores(inputs[0], inputs[1])[0]
        return (jnp.maximum(running, lax.optimization_barrier(jnp.max(scores, axis=2))), None)
    peak = lax.scan(peak_step, jnp.full((HEADS, LATENTS), NEG_BIG, jnp.float32), (normed_all, valid_all))[0]

    def sum_step(running, inputs):
        scores, value_rows = block_scores(inputs[0], inputs[1])
        weights = jnp.exp(scores - peak[:, :, None]) * inputs[1][None, None, :]
        rounded = lax.optimization_barrier(weights.astype(jnp.bfloat16)).astype(jnp.float32)
        totals = running[0] + lax.optimization_barrier(jnp.sum(weights, axis=2))
        weighted = running[1] + jnp.einsum('hlt,thd->hld', rounded, value_rows, precision=lax.Precision.HIGHEST)
        return ((totals, weighted), None)
    start_sums = (jnp.zeros((HEADS, LATENTS), jnp.float32), jnp.zeros((HEADS, LATENTS, HEAD_DIM), jnp.float32))
    totals, weighted = lax.scan(sum_step, start_sums, (normed_all, valid_all))[0]
    pooled = weighted / totals[:, :, None]
    return pooled.transpose(1, 0, 2).reshape(LATENTS, DL).astype(jnp.bfloat16)
```

```python
import jax
import jax.numpy as jnp
from jax import lax
from jax.experimental import pallas as pl
from jax.experimental.pallas import tpu as pltpu
from jax.sharding import PartitionSpec as P

HEAD_DIM = 64
NEG_BIG = -1e30
LN_EPS = 1e-05
F32 = jnp.float32
BF16 = jnp.bfloat16
VMEM = pltpu.VMEM
SMEM = pltpu.SMEM
MIB = 1 << 20


def vmem_spec():
    return pl.BlockSpec(memory_space=VMEM)


def smem_spec():
    return pl.BlockSpec(memory_space=SMEM)


def expand_weights(flat, in_group, out_group, dense_ref):
    groups = flat.shape[0] // (9 * in_group)
    wide = groups * out_group
    source = lax.broadcasted_iota(jnp.int32, (out_group, wide), 0)
    target = lax.broadcasted_iota(jnp.int32, (out_group, wide), 1)
    spread = (lax.rem(target, out_group) == source).astype(BF16)
    tiled = jnp.dot(flat, spread, preferred_element_type=F32)
    row = lax.broadcasted_iota(jnp.int32, tiled.shape, 0)
    lane = lax.broadcasted_iota(jnp.int32, tiled.shape, 1)
    own = lax.div(row, 9 * in_group) == lax.div(lane, out_group)
    tiled = jnp.where(own, tiled, 0.0).astype(BF16)
    dense_ref[...] = jnp.zeros_like(dense_ref)
    for group in range(groups):
        for tap_row in range(3):
            for tap_col in range(3):
                py, px = int(tap_row != 1), int(tap_col != 1)
                block = 2 * int(tap_row == 0) + int(tap_col == 0)
                first = (9 * group + 3 * tap_row + tap_col) * in_group
                to_row = (2 * py + px) * groups * in_group + group * in_group
                dense_ref[pl.ds(to_row, in_group), pl.ds(block * wide, wide)] = tiled[
                    first : first + in_group
                ]


def shifted_down(x):
    row = lax.broadcasted_iota(jnp.int32, x.shape, 0)
    return jnp.where(row == 0, 0.0, pltpu.roll(x, 1, 0))


def stem_kernel(side, count_ref, adjacency_ref, w_ref, pixels_hbm, cells_ref, border_ref,
                pixels, stem, sems):
    chunk_n = sems.shape[0]
    rows = pixels.shape[0] // chunk_n
    copies = [
        pltpu.make_async_copy(
            pixels_hbm.at[0, pl.ds(k * rows, rows)], pixels.at[pl.ds(k * rows, rows)], sems.at[k]
        )
        for k in range(chunk_n)
    ]
    for copy in copies:
        copy.start()
    live = (count_ref[0] > 0).astype(F32)
    weight = w_ref[...]
    channels = weight.shape[1]
    doubled = jnp.concatenate([weight, weight], axis=1)
    half = side // 2
    lane = lax.broadcasted_iota(jnp.int32, (half, 2 * channels), 1)
    left = lane < channels
    lines = rows // side
    for k in range(chunk_n):
        copies[k].wait()
        out = jnp.dot(pixels[pl.ds(k * rows, rows)], doubled, preferred_element_type=F32)
        stem[pl.ds(k * rows, rows)] = jnp.maximum(out, 0.0) * live
        for y in range(k * lines, (k + 1) * lines):
            even = stem[pl.ds(y * side, half, stride=2)]
            odd = stem[pl.ds(y * side + 1, half, stride=2)]
            cells_ref[pl.ds((y // 2) * half, half), pl.ds((y % 2) * 2 * channels, 2 * channels)] = (
                jnp.where(left, even, odd).astype(BF16)
            )
    border_ref[pl.ds(0, 2 * half)] = cells_ref[pl.ds((half - 2) * half, 2 * half)]
    for which in range(2):
        x = side - 4 + 2 * which
        for py in range(2):
            even = stem[pl.ds(py * side + x, half, stride=2 * side)]
            odd = stem[pl.ds(py * side + x + 1, half, stride=2 * side)]
            border_ref[
                pl.ds((2 + which) * half, half), pl.ds(py * 2 * channels, 2 * channels)
            ] = jnp.where(left, even, odd).astype(BF16)
    facts = border_ref.shape[0] - 4 * half
    row = lax.broadcasted_iota(jnp.int32, (facts, border_ref.shape[1]), 0)
    above = (adjacency_ref[0, 0] == 0).astype(F32)
    beside = (adjacency_ref[0, 1] == 0).astype(F32)
    told = jnp.where(row == 0, live, jnp.where(row == 1, above, jnp.where(row == 2, beside, 0.0)))
    border_ref[pl.ds(4 * half, facts)] = told.astype(BF16)


def conv_kernel(half, in_group, cells_ref, w1_ref, w2_ref, partial_ref, dense1_ref, dense2_ref,
                wide):
    expand_weights(w1_ref[...], in_group, w1_ref.shape[1], dense1_ref)
    positions, channels = partial_ref.shape
    chunk = 8 * half
    wide[pl.ds(0, half)] = jnp.zeros((half, wide.shape[1]), F32)
    row = lax.broadcasted_iota(jnp.int32, (chunk, channels), 0)
    first = lax.rem(row, half) == 0
    dense = dense1_ref[...]
    for k in range(positions // chunk):
        wide[pl.ds(half + k * chunk, chunk)] = jnp.dot(
            cells_ref[pl.ds(k * chunk, chunk)], dense, preferred_element_type=F32
        )
        here = pl.ds(half + k * chunk, chunk)
        up = pl.ds(k * chunk, chunk)
        lane = [pl.ds(b * channels, channels) for b in range(4)]
        before = wide[here, lane[1]] + wide[up, lane[3]]
        before = jnp.where(first, 0.0, pltpu.roll(before, 1, 0))
        partial_ref[pl.ds(k * chunk, chunk)] = wide[here, lane[0]] + wide[up, lane[2]] + before
    expand_weights(w2_ref[...], w2_ref.shape[0] // 36, w2_ref.shape[1], dense2_ref)


def token_kernel(count_ref, tissue_ref, adjacency_ref, partial_ref, prior_ref, second_ref,
                 dense1_ref, dense2_ref, token_ref, middle, lines, cells, wide, whole):
    positions, channels = partial_ref.shape
    half = 32
    while half * half > positions:
        half //= 2
    quarter = half // 2
    live = (count_ref[0] > 0).astype(F32)
    above = (adjacency_ref[0, 0] == 0).astype(F32)
    beside = (adjacency_ref[0, 1] == 0).astype(F32)
    corner = (adjacency_ref[0, 2] == 0).astype(F32)
    lane = [slice(b * channels, (b + 1) * channels) for b in range(4)]
    dense1 = dense1_ref[...]
    prior = jnp.dot(prior_ref[pl.ds(0, 4 * half)], dense1, preferred_element_type=F32)
    second = jnp.dot(second_ref[pl.ds(0, 2 * half)], dense1, preferred_element_type=F32)
    facts = prior_ref[pl.ds(4 * half, 16), pl.ds(0, channels)].astype(F32)
    live_prior, above_prior, beside_prior = facts[0:1], facts[1:2], facts[2:3]
    row_30 = prior[0:half]
    row_31 = prior[half : 2 * half]
    col_30 = prior[2 * half : 3 * half]
    col_31 = prior[3 * half : 4 * half]
    at_zero = lax.broadcasted_iota(jnp.int32, (half, channels), 0) == 0
    middle[...] = jnp.maximum(partial_ref[...], 0.0) * live
    top = above * (row_31[:, lane[2]] + shifted_down(row_31[:, lane[3]]))
    top = top + jnp.where(at_zero, corner * row_31[half - 1 : half, lane[3]], 0.0)
    side = beside * (col_31[:, lane[1]] + shifted_down(col_31[:, lane[3]]))
    top_sum = partial_ref[pl.ds(0, half)] + top
    side_sum = partial_ref[pl.ds(0, half, stride=half)] + side
    side_sum = side_sum + jnp.where(at_zero, top, 0.0)
    middle[pl.ds(0, half)] = jnp.maximum(top_sum, 0.0) * live
    middle[pl.ds(0, half, stride=half)] = jnp.maximum(side_sum, 0.0) * live
    last = second[2 * half - 1 : 2 * half]
    over_last = second[half - 1 : half]
    left_last = second[2 * half - 2 : 2 * half - 1]
    row_sum = row_31[:, lane[0]] + row_30[:, lane[2]]
    row_sum = row_sum + shifted_down(row_31[:, lane[1]] + row_30[:, lane[3]])
    row_sum = row_sum + jnp.where(
        at_zero, beside_prior * (last[:, lane[1]] + over_last[:, lane[3]]), 0.0
    )
    col_sum = col_31[:, lane[0]] + col_30[:, lane[1]]
    col_sum = col_sum + shifted_down(col_31[:, lane[2]] + col_30[:, lane[3]])
    col_sum = col_sum + jnp.where(
        at_zero, above_prior * (last[:, lane[2]] + left_last[:, lane[3]]), 0.0
    )
    lines[pl.ds(0, half)] = jnp.maximum(row_sum, 0.0) * live_prior
    lines[pl.ds(half, half)] = jnp.maximum(col_sum, 0.0) * live_prior
    for i in range(half):
        for px in range(2):
            cells[
                pl.ds((i // 2) * quarter, quarter), pl.ds((2 * (i % 2) + px) * channels, channels)
            ] = middle[pl.ds(i * half + px, quarter, stride=2)].astype(BF16)
    tokens = quarter * quarter
    cells[pl.ds(tokens, 2 * quarter)] = jnp.zeros((2 * quarter, cells.shape[1]), BF16)
    for parity in range(2):
        cells[pl.ds(tokens, quarter), pl.ds((2 + parity) * channels, channels)] = lines[
            pl.ds(parity, quarter, stride=2)
        ].astype(BF16)
        cells[pl.ds(tokens + quarter, quarter), pl.ds((2 * parity + 1) * channels, channels)] = (
            lines[pl.ds(half + parity, quarter, stride=2)].astype(BF16)
        )
    out_n = dense2_ref.shape[1] // 4
    wide[...] = jnp.dot(cells[...], dense2_ref[...], preferred_element_type=F32)
    block = [pl.ds(b * out_n, out_n) for b in range(4)]
    body, up = pl.ds(quarter, tokens - quarter), pl.ds(0, tokens - quarter)
    topmost = pl.ds(0, quarter)
    above_rows, beside_rows = pl.ds(tokens, quarter), pl.ds(tokens + quarter, quarter)
    at_zero = lax.broadcasted_iota(jnp.int32, (quarter, out_n), 0) == 0
    wide[body, block[0]] = wide[body, block[0]] + wide[up, block[2]]
    wide[topmost, block[0]] = wide[topmost, block[0]] + above * wide[above_rows, block[2]]
    before = wide[pl.ds(0, tokens), block[1]]
    up_left = jnp.concatenate(
        [above * wide[above_rows, block[3]], wide[up, block[3]]], axis=0
    )
    before = before + up_left
    row = lax.broadcasted_iota(jnp.int32, before.shape, 0)
    before = jnp.where(lax.rem(row, quarter) == 0, 0.0, pltpu.roll(before, 1, 0))
    deep = wide[pl.ds(0, tokens), block[0]] + before
    left = beside * (wide[beside_rows, block[1]] + shifted_down(wide[beside_rows, block[3]]))
    left = left + jnp.where(
        at_zero, corner * wide[pl.ds(tokens + quarter - 1, 1), block[3]], 0.0
    )
    spots = pl.ds(0, quarter, stride=quarter)
    pieces = []
    for part in range(out_n // 128):
        column = slice(part * 128, (part + 1) * 128)
        whole[part] = deep[:, column]
        whole[part, spots] = whole[part, spots] + left[:, column]
        pieces.append(whole[part])
    deep = jnp.maximum(jnp.concatenate(pieces, axis=1), 0.0)
    centred = deep - jnp.mean(deep, axis=1, keepdims=True)
    spread = jnp.mean(centred * centred, axis=1, keepdims=True)
    token_ref[pl.ds(0, tokens)] = (centred * lax.rsqrt(spread + LN_EPS)).astype(BF16)
    known = (live * tissue_ref[0].astype(F32)) * jnp.ones((16, out_n), F32)
    token_ref[pl.ds(tokens, 16)] = known.astype(BF16)


def attention_kernel(place_ref, t0, t1, t2, t3, wk_ref, wv_ref, q_ref, out_ref, keys, values):
    token_refs = (t0, t1, t2, t3)
    tokens = t0.shape[0] - 16
    width = wk_ref.shape[1]
    both = jnp.concatenate([wk_ref[...], wv_ref[...]], axis=1)
    masks = []
    lane_token = lax.broadcasted_iota(jnp.int32, (1, tokens), 1).astype(F32)
    for b, ref in enumerate(token_refs):
        made = jnp.dot(ref[pl.ds(0, tokens)], both, preferred_element_type=F32).astype(BF16)
        keys[pl.ds(b * tokens, tokens)] = made[:, :width]
        values[pl.ds(b * tokens, tokens)] = made[:, width:]
        known = ref[pl.ds(tokens, 16), pl.ds(0, tokens)].astype(F32)[0:1]
        masks.append(jnp.where(lane_token < known, 0.0, NEG_BIG))
    bias = jnp.concatenate(masks, axis=1)
    place = place_ref[0]
    part_n, part_rows = out_ref.shape[0], out_ref.shape[1] - 16
    lane = lax.broadcasted_iota(jnp.int32, (part_rows, width), 1)
    row8 = lax.broadcasted_iota(jnp.int32, (8, part_rows), 0)
    key_all = keys[...]
    value_all = values[...]
    for k in range(part_n):
        part = place ^ k
        q = q_ref[pl.ds(pl.multiple_of(part * part_rows, part_rows), part_rows)].astype(F32)
        q = q * (float(HEAD_DIM) ** -0.5)
        joined = None
        facts = jnp.zeros((part_rows, width), F32)
        head_n = width // HEAD_DIM
        for h in range(head_n):
            mine = lax.div(lane, HEAD_DIM) == h
            q_h = jnp.where(mine, q, 0.0).astype(BF16)
            scores = lax.dot_general(
                q_h, key_all, (((1,), (1,)), ((), ())), preferred_element_type=F32
            )
            scores = scores + bias
            peak = jnp.max(scores, axis=1, keepdims=True)
            weights = jnp.exp(scores - peak)
            total = jnp.sum(weights, axis=1, keepdims=True)
            summed = jnp.dot(weights.astype(BF16), value_all, preferred_element_type=F32)
            joined = summed if joined is None else jnp.where(mine, summed, joined)
            facts = jnp.where(lane == h, peak, facts)
            facts = jnp.where(lane == head_n + h, total, facts)
        out_ref[k, pl.ds(0, part_rows)] = joined.astype(BF16)
        turned = facts.T[0:8]
        high = turned.astype(BF16).astype(F32)
        rest = turned - high
        mid = rest.astype(BF16).astype(F32)
        low = rest - mid
        upper = jnp.where(row8 < 4, high, pltpu.roll(mid, 4, 0))
        out_ref[k, pl.ds(part_rows, 16)] = jnp.concatenate([upper, low], axis=0).astype(BF16)


def merge_kernel(head_n, m0, m1, m2, m3, out_ref):
    part_rows = out_ref.shape[0]
    width = out_ref.shape[1]
    stats = []
    for ref in (m0, m1, m2, m3):
        coded = ref[pl.ds(part_rows, 16)].astype(F32)
        upper, low = coded[0:8], coded[8:16]
        stats.append(upper + pltpu.roll(upper, 4, 0) + low)
    row8 = lax.broadcasted_iota(jnp.int32, stats[0].shape, 0)
    peak = jnp.maximum(jnp.maximum(stats[0], stats[1]), jnp.maximum(stats[2], stats[3]))
    scales = [jnp.exp(jnp.where(row8 < head_n, s - peak, 0.0)) for s in stats]
    totals = [c * pltpu.roll(s, 8 - head_n, 0) for c, s in zip(scales, stats)]
    total = totals[0] + totals[1] + totals[2] + totals[3]
    total = jnp.where(row8 < head_n, total, 1.0)
    scales = [c / total for c in scales]
    packed = jnp.concatenate(scales + [jnp.zeros((part_rows - 32, part_rows), F32)], axis=0)
    turned = packed.T
    lane = lax.broadcasted_iota(jnp.int32, (part_rows, width), 1)
    result = jnp.zeros((part_rows, width), F32)
    for k, ref in enumerate((m0, m1, m2, m3)):
        scale = jnp.broadcast_to(turned[:, 8 * k : 8 * k + 1], (part_rows, width))
        for h in range(1, head_n):
            scale = jnp.where(
                lax.div(lane, HEAD_DIM) == h, turned[:, 8 * k + h : 8 * k + h + 1], scale
            )
        result = result + ref[pl.ds(0, part_rows)].astype(F32) * scale
    out_ref[...] = result.astype(BF16)


def swapped(x, axis, distance):
    return lax.ppermute(x, axis, [(i, i ^ distance) for i in range(lax.axis_size(axis))])


def per_device(
    pixels, w_stem, w_conv1, w_conv2, w_key, w_value, queries, tile_count, tissue, adjacency
):
    slot_n, area, patch = pixels.shape
    assert slot_n == 1
    side = int(round(area**0.5))
    half, quarter = side // 2, side // 4
    channels = w_stem.shape[1]
    groups, _, in1, out1 = w_conv1.shape
    _, _, in2, out2 = w_conv2.shape
    mid_n, out_n = groups * out1, groups * out2
    tokens = quarter * quarter
    border_rows = 4 * half + 16
    chunk_n = 4

    cells, border = pl.pallas_call(
        lambda *refs: stem_kernel(side, *refs),
        name="stem",
        out_shape=(
            jax.ShapeDtypeStruct((half * half, 4 * channels), BF16),
            jax.ShapeDtypeStruct((border_rows, 4 * channels), BF16),
        ),
        in_specs=[smem_spec(), smem_spec(), vmem_spec(), pl.BlockSpec(memory_space=pl.ANY)],
        out_specs=(vmem_spec(), vmem_spec()),
        scratch_shapes=[
            VMEM((area, patch), BF16),
            VMEM((area, 2 * channels), F32),
            pltpu.SemaphoreType.DMA((chunk_n,)),
        ],
        compiler_params=pltpu.CompilerParams(vmem_limit_bytes=20 * MIB),
    )(tile_count, adjacency, w_stem, pixels)

    line = ("tiles", "heads")
    line_n = lax.axis_size("tiles") * lax.axis_size("heads")
    second = lax.ppermute(border, line, [(i, i + 2) for i in range(line_n - 2)])
    partial, dense1, dense2 = pl.pallas_call(
        lambda *refs: conv_kernel(half, in1, *refs),
        name="conv",
        out_shape=(
            jax.ShapeDtypeStruct((half * half, mid_n), F32),
            jax.ShapeDtypeStruct((4 * channels, 4 * mid_n), BF16),
            jax.ShapeDtypeStruct((4 * mid_n, 4 * out_n), BF16),
        ),
        in_specs=[vmem_spec()] * 3,
        out_specs=(vmem_spec(),) * 3,
        scratch_shapes=[VMEM((half * half + half, 4 * mid_n), F32)],
        compiler_params=pltpu.CompilerParams(vmem_limit_bytes=20 * MIB),
        cost_estimate=pl.CostEstimate(flops=10**9, bytes_accessed=4 * 10**6, transcendentals=0),
    )(cells, w_conv1.reshape(groups * 9 * in1, out1), w_conv2.reshape(groups * 9 * in2, out2))

    odd = lax.rem(lax.axis_index(line), 2) == 1
    prior = lax.ppermute(
        jnp.where(odd, second, border), line, [(i, i ^ 1) for i in range(line_n)]
    )
    message = pl.pallas_call(
        token_kernel,
        name="token",
        out_shape=jax.ShapeDtypeStruct((tokens + 16, out_n), BF16),
        in_specs=[smem_spec()] * 3 + [vmem_spec()] * 5,
        out_specs=vmem_spec(),
        scratch_shapes=[
            VMEM((half * half, mid_n), F32),
            VMEM((2 * half, mid_n), F32),
            VMEM((tokens + 2 * quarter, 4 * mid_n), BF16),
            VMEM((tokens + 2 * quarter, 4 * out_n), F32),
            VMEM((out_n // 128, tokens, 128), F32),
        ],
        compiler_params=pltpu.CompilerParams(vmem_limit_bytes=20 * MIB),
    )(tile_count, tissue, adjacency, partial, prior, second, dense1, dense2)

    far = swapped(message, "heads", 2)
    near = swapped(message, "heads", 1)
    far_near = swapped(far, "heads", 1)

    tile_n = lax.axis_size("tiles")
    latent_n, width = queries.shape
    head_n = width // HEAD_DIM
    share = latent_n // tile_n
    few = tile_n == 4
    part_n = 4
    part_rows = latent_n // part_n
    place = lax.axis_index("tiles") if few else jnp.int32(0)
    parts = pl.pallas_call(
        attention_kernel,
        name="attention",
        out_shape=jax.ShapeDtypeStruct((part_n, part_rows + 16, width), BF16),
        in_specs=[smem_spec()] + [vmem_spec()] * 7,
        out_specs=vmem_spec(),
        scratch_shapes=[VMEM((4 * tokens, width), BF16), VMEM((4 * tokens, width), BF16)],
        compiler_params=pltpu.CompilerParams(vmem_limit_bytes=24 * MIB),
    )(place.astype(jnp.int32).reshape(1), message, near, far, far_near, w_key, w_value, queries)

    if few:
        received = [parts[0]] + [swapped(parts[k], "tiles", k) for k in range(1, 4)]
        return pl.pallas_call(
            lambda *refs: merge_kernel(head_n, *refs),
            name="merge",
            out_shape=jax.ShapeDtypeStruct((part_rows, width), BF16),
            in_specs=[vmem_spec()] * 4,
            out_specs=vmem_spec(),
        )(*received)
    coded = parts[:, part_rows:].astype(F32)
    stats = coded[:, 0:4] + coded[:, 4:8] + coded[:, 8:12]
    stats = stats.transpose(0, 2, 1).reshape(tile_n, share, 4)
    weighted = parts[:, :part_rows].reshape(tile_n, share, width)
    stats = lax.all_to_all(stats, "tiles", 0, 0)
    weighted = lax.all_to_all(weighted, "tiles", 0, 0).astype(F32)
    peaks, totals = stats[..., :head_n], stats[..., head_n : 2 * head_n]
    scale = jnp.exp(peaks - jnp.max(peaks, axis=0, keepdims=True))
    scale = scale / jnp.sum(scale * totals, axis=0, keepdims=True)
    return jnp.sum(weighted * jnp.repeat(scale, HEAD_DIM, axis=2), axis=0).astype(BF16)


def solution(mesh):
    in_specs = (
        P(("slides", "tiles", "heads"), None, None),
        P(),
        P(),
        P(),
        P(None, "heads"),
        P(None, "heads"),
        P(None, "heads"),
        P(("slides", "tiles", "heads")),
        P(("slides", "tiles", "heads")),
        P(("slides", "tiles", "heads"), None),
    )
    out_specs = P(("slides", "tiles"), "heads")
    return jax.shard_map(
        per_device, mesh=mesh, in_specs=in_specs, out_specs=out_specs, check_vma=False
    )
```

```python
import jax
import jax.numpy as jnp
from jax import lax
from jax.experimental import pallas as pl
from jax.experimental.pallas import tpu as pltpu
from jax.sharding import PartitionSpec as P

HEAD_DIM = 64
NEG_BIG = -1e30
LN_EPS = 1e-05
F32 = jnp.float32
BF16 = jnp.bfloat16
VMEM = pltpu.VMEM
SMEM = pltpu.SMEM
MIB = 1 << 20
STEM_VMEM = 60 * MIB


def vmem_spec():
    return pl.BlockSpec(memory_space=VMEM)


def smem_spec():
    return pl.BlockSpec(memory_space=SMEM)


def expand_weights(flat, in_group, out_group, dense_ref):
    groups = flat.shape[0] // (9 * in_group)
    wide = groups * out_group
    source = lax.broadcasted_iota(jnp.int32, (out_group, wide), 0)
    target = lax.broadcasted_iota(jnp.int32, (out_group, wide), 1)
    spread = (lax.rem(target, out_group) == source).astype(BF16)
    tiled = jnp.dot(flat, spread, preferred_element_type=F32)
    row = lax.broadcasted_iota(jnp.int32, tiled.shape, 0)
    lane = lax.broadcasted_iota(jnp.int32, tiled.shape, 1)
    own = lax.div(row, 9 * in_group) == lax.div(lane, out_group)
    tiled = jnp.where(own, tiled, 0.0).astype(BF16)
    dense_ref[...] = jnp.zeros_like(dense_ref)
    for group in range(groups):
        for tap_row in range(3):
            for tap_col in range(3):
                py, px = int(tap_row != 1), int(tap_col != 1)
                block = 2 * int(tap_row == 0) + int(tap_col == 0)
                first = (9 * group + 3 * tap_row + tap_col) * in_group
                to_row = (2 * py + px) * groups * in_group + group * in_group
                dense_ref[pl.ds(to_row, in_group), pl.ds(block * wide, wide)] = tiled[
                    first : first + in_group
                ]


def shifted_down(x):
    row = lax.broadcasted_iota(jnp.int32, x.shape, 0)
    return jnp.where(row == 0, 0.0, pltpu.roll(x, 1, 0))


def stem_kernel(side, count_any, tissue_any, adjacency_any, w_any, pixels_any, cells_ref,
                border_ref, tiny_ref, facts_ref, count, tissue, adjacency, weight, pixels,
                even_lines, odd_lines, sems):
    copies = [
        pltpu.make_async_copy(source, target, sems.at[k])
        for k, (source, target) in enumerate((
            (pixels_any, pixels), (w_any, weight), (count_any, count), (tissue_any, tissue),
            (adjacency_any, adjacency),
        ))
    ]
    for copy in copies:
        copy.start()
    channels, half = weight.shape[0], side // 2
    rows, span = 4 * half, 4 * side
    row = lax.broadcasted_iota(jnp.int32, (rows, 2 * span), 0)
    column = lax.broadcasted_iota(jnp.int32, (rows, 2 * span), 1)
    line = 2 * lax.div(lax.rem(row, 2 * half), half) + lax.div(row, 2 * half)
    wanted = line * side + 2 * lax.rem(row, half)
    pick = (lax.rem(column, span) == wanted + lax.div(column, span)).astype(BF16)
    for copy in copies:
        copy.wait()
    live = (count[0, 0] > 0).astype(F32)
    gates = [(adjacency[0, k] == 0).astype(F32) for k in range(3)]
    row = lax.broadcasted_iota(jnp.int32, facts_ref.shape, 0)
    facts = jnp.zeros(facts_ref.shape, F32)
    for k, fact in enumerate([live] + gates + [live * tissue[0, 0].astype(F32)]):
        facts = jnp.where(row == k, fact, facts)
    facts_ref[...] = facts.astype(BF16)
    flat = jnp.dot(weight[...], pixels[0], preferred_element_type=F32)
    flat = (jnp.maximum(flat, 0.0) * live).astype(BF16)
    blank = jnp.zeros((channels, span), BF16)
    for k in range(side // 4):
        four = flat[:, k * span : (k + 1) * span]
        both = jnp.concatenate(
            [jnp.concatenate([four, blank], axis=0), jnp.concatenate([blank, four], axis=0)],
            axis=1,
        )
        sorted_ = lax.dot_general(
            pick, both, (((1,), (1,)), ((), ())), preferred_element_type=F32
        )
        here = pl.ds(k * 2 * half, 2 * half)
        even_lines[here] = sorted_[: 2 * half]
        odd_lines[here] = sorted_[2 * half :]
        cells_ref[here, pl.ds(0, 2 * channels)] = sorted_[: 2 * half].astype(BF16)
        cells_ref[here, pl.ds(2 * channels, 2 * channels)] = sorted_[2 * half :].astype(BF16)
    border_ref[pl.ds(0, 2 * half)] = cells_ref[pl.ds((half - 2) * half, 2 * half)]
    for which in range(2):
        for py, lines in enumerate((even_lines, odd_lines)):
            border_ref[
                pl.ds((2 + which) * half, half), pl.ds(py * 2 * channels, 2 * channels)
            ] = lines[pl.ds(half - 2 + which, half, stride=half)].astype(BF16)
    border_ref[pl.ds(4 * half, 16)] = facts_ref[...]
    tiny_ref[pl.ds(0, 16)] = cells_ref[pl.ds((half - 1) * half - 16, 16)]
    tiny_ref[pl.ds(16, 16)] = cells_ref[pl.ds(half * half - 16, 16)]


def conv_kernel(half, in_group, cells_ref, w1_ref, w2_ref, partial_ref, dense1_ref, dense2_ref,
                wide):
    expand_weights(w1_ref[...], in_group, w1_ref.shape[1], dense1_ref)
    positions, channels = partial_ref.shape
    chunk = 8 * half
    wide[pl.ds(0, half)] = jnp.zeros((half, wide.shape[1]), F32)
    row = lax.broadcasted_iota(jnp.int32, (chunk, channels), 0)
    first = lax.rem(row, half) == 0
    dense = dense1_ref[...]
    for k in range(positions // chunk):
        wide[pl.ds(half + k * chunk, chunk)] = jnp.dot(
            cells_ref[pl.ds(k * chunk, chunk)], dense, preferred_element_type=F32
        )
        here = pl.ds(half + k * chunk, chunk)
        up = pl.ds(k * chunk, chunk)
        lane = [pl.ds(b * channels, channels) for b in range(4)]
        before = wide[here, lane[1]] + wide[up, lane[3]]
        before = jnp.where(first, 0.0, pltpu.roll(before, 1, 0))
        partial_ref[pl.ds(k * chunk, chunk)] = wide[here, lane[0]] + wide[up, lane[2]] + before
    expand_weights(w2_ref[...], w2_ref.shape[0] // 36, w2_ref.shape[1], dense2_ref)


def token_kernel(facts_ref, partial_ref, prior_ref, second_ref, dense1_ref,
                 dense2_ref, token_ref, middle, lines, cells, wide, whole):
    positions, channels = partial_ref.shape
    half = 32
    while half * half > positions:
        half //= 2
    quarter = half // 2
    live, above, beside, corner, known = [
        facts_ref[pl.ds(0, 16), pl.ds(0, 1)].astype(F32)[k : k + 1] for k in range(5)
    ]
    lane = [slice(b * channels, (b + 1) * channels) for b in range(4)]
    dense1 = dense1_ref[...]
    prior = jnp.dot(prior_ref[pl.ds(0, 4 * half)], dense1, preferred_element_type=F32)
    second = jnp.dot(second_ref[...], dense1, preferred_element_type=F32)
    facts = prior_ref[pl.ds(4 * half, 16), pl.ds(0, channels)].astype(F32)
    live_prior, above_prior, beside_prior = facts[0:1], facts[1:2], facts[2:3]
    row_30 = prior[0:half]
    row_31 = prior[half : 2 * half]
    col_30 = prior[2 * half : 3 * half]
    col_31 = prior[3 * half : 4 * half]
    at_zero = lax.broadcasted_iota(jnp.int32, (half, channels), 0) == 0
    middle[...] = jnp.maximum(partial_ref[...], 0.0) * live
    top = above * (row_31[:, lane[2]] + shifted_down(row_31[:, lane[3]]))
    top = top + jnp.where(at_zero, corner * row_31[half - 1 : half, lane[3]], 0.0)
    side = beside * (col_31[:, lane[1]] + shifted_down(col_31[:, lane[3]]))
    top_sum = partial_ref[pl.ds(0, half)] + top
    side_sum = partial_ref[pl.ds(0, half, stride=half)] + side
    side_sum = side_sum + jnp.where(at_zero, top, 0.0)
    middle[pl.ds(0, half)] = jnp.maximum(top_sum, 0.0) * live
    middle[pl.ds(0, half, stride=half)] = jnp.maximum(side_sum, 0.0) * live
    over_last, left_last, last = second[15:16], second[30:31], second[31:32]
    row_sum = row_31[:, lane[0]] + row_30[:, lane[2]]
    row_sum = row_sum + shifted_down(row_31[:, lane[1]] + row_30[:, lane[3]])
    row_sum = row_sum + jnp.where(
        at_zero, beside_prior * (last[:, lane[1]] + over_last[:, lane[3]]), 0.0
    )
    col_sum = col_31[:, lane[0]] + col_30[:, lane[1]]
    col_sum = col_sum + shifted_down(col_31[:, lane[2]] + col_30[:, lane[3]])
    col_sum = col_sum + jnp.where(
        at_zero, above_prior * (last[:, lane[2]] + left_last[:, lane[3]]), 0.0
    )
    lines[pl.ds(0, half)] = jnp.maximum(row_sum, 0.0) * live_prior
    lines[pl.ds(half, half)] = jnp.maximum(col_sum, 0.0) * live_prior
    for i in range(half):
        for px in range(2):
            cells[
                pl.ds((i // 2) * quarter, quarter), pl.ds((2 * (i % 2) + px) * channels, channels)
            ] = middle[pl.ds(i * half + px, quarter, stride=2)].astype(BF16)
    tokens = quarter * quarter
    cells[pl.ds(tokens, 2 * quarter)] = jnp.zeros((2 * quarter, cells.shape[1]), BF16)
    for parity in range(2):
        cells[pl.ds(tokens, quarter), pl.ds((2 + parity) * channels, channels)] = lines[
            pl.ds(parity, quarter, stride=2)
        ].astype(BF16)
        cells[pl.ds(tokens + quarter, quarter), pl.ds((2 * parity + 1) * channels, channels)] = (
            lines[pl.ds(half + parity, quarter, stride=2)].astype(BF16)
        )
    out_n = dense2_ref.shape[1] // 4
    wide[...] = jnp.dot(cells[...], dense2_ref[...], preferred_element_type=F32)
    block = [pl.ds(b * out_n, out_n) for b in range(4)]
    body, up = pl.ds(quarter, tokens - quarter), pl.ds(0, tokens - quarter)
    topmost = pl.ds(0, quarter)
    above_rows, beside_rows = pl.ds(tokens, quarter), pl.ds(tokens + quarter, quarter)
    at_zero = lax.broadcasted_iota(jnp.int32, (quarter, out_n), 0) == 0
    wide[body, block[0]] = wide[body, block[0]] + wide[up, block[2]]
    wide[topmost, block[0]] = wide[topmost, block[0]] + above * wide[above_rows, block[2]]
    before = wide[pl.ds(0, tokens), block[1]]
    up_left = jnp.concatenate(
        [above * wide[above_rows, block[3]], wide[up, block[3]]], axis=0
    )
    before = before + up_left
    row = lax.broadcasted_iota(jnp.int32, before.shape, 0)
    before = jnp.where(lax.rem(row, quarter) == 0, 0.0, pltpu.roll(before, 1, 0))
    deep = wide[pl.ds(0, tokens), block[0]] + before
    left = beside * (wide[beside_rows, block[1]] + shifted_down(wide[beside_rows, block[3]]))
    left = left + jnp.where(
        at_zero, corner * wide[pl.ds(tokens + quarter - 1, 1), block[3]], 0.0
    )
    spots = pl.ds(0, quarter, stride=quarter)
    pieces = []
    for part in range(out_n // 128):
        column = slice(part * 128, (part + 1) * 128)
        whole[part] = deep[:, column]
        whole[part, spots] = whole[part, spots] + left[:, column]
        pieces.append(whole[part])
    deep = jnp.maximum(jnp.concatenate(pieces, axis=1), 0.0)
    centred = deep - jnp.mean(deep, axis=1, keepdims=True)
    spread = jnp.mean(centred * centred, axis=1, keepdims=True)
    token_ref[pl.ds(0, tokens)] = (centred * lax.rsqrt(spread + LN_EPS)).astype(BF16)
    token_ref[pl.ds(tokens, 16)] = jnp.broadcast_to(known, (16, out_n)).astype(BF16)


def attention_kernel(place_ref, t0, t1, t2, t3, wk_ref, wv_ref, q_ref, *rest):
    out_refs, (keys, values, sums, facts_all) = rest[:-4], rest[-4:]
    token_refs = (t0, t1, t2, t3)
    tokens = t0.shape[0] - 16
    latent_n, width = q_ref.shape
    head_n = width // HEAD_DIM
    both = jnp.concatenate([wk_ref[...], wv_ref[...]], axis=1)
    masks = []
    lane_token = lax.broadcasted_iota(jnp.int32, (1, tokens), 1).astype(F32)
    for b, ref in enumerate(token_refs):
        made = jnp.dot(ref[pl.ds(0, tokens)], both, preferred_element_type=F32).astype(BF16)
        keys[pl.ds(b * tokens, tokens)] = made[:, :width]
        values[pl.ds(b * tokens, tokens)] = made[:, width:]
        known = ref[pl.ds(tokens, 16), pl.ds(0, tokens)].astype(F32)[0:1]
        masks.append(jnp.where(lane_token < known, 0.0, NEG_BIG))
    bias = jnp.concatenate(masks, axis=1)
    part_rows = latent_n // len(out_refs)
    lane = lax.broadcasted_iota(jnp.int32, (part_rows, width), 1)
    key_all = keys[...]
    value_all = values[...]
    for k in range(len(out_refs)):
        here = pl.ds(k * part_rows, part_rows)
        q = q_ref[here].astype(F32) * (float(HEAD_DIM) ** -0.5)
        q = jnp.concatenate(
            [jnp.where(lax.div(lane, HEAD_DIM) == h, q, 0.0) for h in range(head_n)], axis=0
        ).astype(BF16)
        scores = lax.dot_general(
            q, key_all, (((1,), (1,)), ((), ())), preferred_element_type=F32
        )
        scores = scores + bias
        peak = jnp.max(scores, axis=1, keepdims=True)
        weights = jnp.exp(scores - peak)
        total = jnp.sum(weights, axis=1, keepdims=True)
        summed = jnp.dot(weights.astype(BF16), value_all, preferred_element_type=F32)
        joined = summed[:part_rows]
        facts = jnp.zeros((part_rows, width), F32)
        for h in range(head_n):
            mine = slice(h * part_rows, (h + 1) * part_rows)
            joined = jnp.where(lax.div(lane, HEAD_DIM) == h, summed[mine], joined)
            facts = jnp.where(lane == h, peak[mine], facts)
            facts = jnp.where(lane == head_n + h, total[mine], facts)
        sums[here] = joined
        facts_all[here] = facts
    for k, out_ref in enumerate(out_refs):
        part = place_ref[0] ^ k
        there = pl.ds(pl.multiple_of(part * part_rows, part_rows), part_rows)
        out_ref[pl.ds(0, part_rows)] = sums[there]
        out_ref[pl.ds(part_rows, 8)] = facts_all[there].T[0:8]


def merge_kernel(head_n, *refs):
    in_refs, out_ref = refs[:-1], refs[-1]
    part_rows, width = out_ref.shape
    stats = [ref[pl.ds(part_rows, 8)] for ref in in_refs]
    row8 = lax.broadcasted_iota(jnp.int32, stats[0].shape, 0)
    peak = stats[0]
    for s in stats[1:]:
        peak = jnp.maximum(peak, s)
    scales = [jnp.exp(jnp.where(row8 < head_n, s - peak, 0.0)) for s in stats]
    total = scales[0] * pltpu.roll(stats[0], 8 - head_n, 0)
    for c, s in zip(scales[1:], stats[1:]):
        total = total + c * pltpu.roll(s, 8 - head_n, 0)
    total = jnp.where(row8 < head_n, total, 1.0)
    scales = [c / total for c in scales]
    blank = jnp.zeros((part_rows - 8 * len(scales), part_rows), F32)
    turned = jnp.concatenate(scales + [blank], axis=0).T
    lane = lax.broadcasted_iota(jnp.int32, (part_rows, width), 1)
    result = jnp.zeros((part_rows, width), F32)
    for k, ref in enumerate(in_refs):
        scale = turned[:, 8 * k : 8 * k + 1]
        for h in range(1, head_n):
            scale = jnp.where(
                lax.div(lane, HEAD_DIM) == h, turned[:, 8 * k + h : 8 * k + h + 1], scale
            )
        result = result + ref[pl.ds(0, part_rows)] * scale
    out_ref[...] = result.astype(BF16)


def swapped(x, axis, distance):
    return lax.ppermute(x, axis, [(i, i ^ distance) for i in range(lax.axis_size(axis))])


def per_device(
    pixels, w_stem, w_conv1, w_conv2, w_key, w_value, queries, tile_count, tissue, adjacency
):
    slot_n, area, patch = pixels.shape
    assert slot_n == 1
    side = int(round(area**0.5))
    half, quarter = side // 2, side // 4
    channels = w_stem.shape[1]
    groups, _, in1, out1 = w_conv1.shape
    _, _, in2, out2 = w_conv2.shape
    mid_n, out_n = groups * out1, groups * out2
    tokens = quarter * quarter
    border_rows = 4 * half + 16

    cells, border, tiny, facts = pl.pallas_call(
        lambda *refs: stem_kernel(side, *refs),
        name="stem",
        out_shape=(
            jax.ShapeDtypeStruct((half * half, 4 * channels), BF16),
            jax.ShapeDtypeStruct((border_rows, 4 * channels), BF16),
            jax.ShapeDtypeStruct((32, 4 * channels), BF16),
            jax.ShapeDtypeStruct((16, 4 * channels), BF16),
        ),
        in_specs=[pl.BlockSpec(memory_space=pl.ANY)] * 5,
        out_specs=(vmem_spec(),) * 4,
        scratch_shapes=[
            SMEM((1, 1), jnp.int32),
            SMEM((1, 1), jnp.int32),
            SMEM((1, 3), jnp.int32),
            VMEM((channels, patch), BF16),
            VMEM((1, patch, area), BF16),
            VMEM((half * half, 2 * channels), F32),
            VMEM((half * half, 2 * channels), F32),
            pltpu.SemaphoreType.DMA((5,)),
        ],
        compiler_params=pltpu.CompilerParams(vmem_limit_bytes=STEM_VMEM),
    )(
        tile_count.reshape(1, 1), tissue.reshape(1, 1), adjacency, w_stem.T,
        jnp.swapaxes(pixels, 1, 2),
    )

    line = ("tiles", "heads")
    line_n = lax.axis_size("tiles") * lax.axis_size("heads")
    prior = lax.ppermute(border, line, [(i, i + 1) for i in range(line_n - 1)])
    second = lax.ppermute(tiny, line, [(i, i + 2) for i in range(line_n - 2)])
    partial, dense1, dense2 = pl.pallas_call(
        lambda *refs: conv_kernel(half, in1, *refs),
        name="conv",
        out_shape=(
            jax.ShapeDtypeStruct((half * half, mid_n), F32),
            jax.ShapeDtypeStruct((4 * channels, 4 * mid_n), BF16),
            jax.ShapeDtypeStruct((4 * mid_n, 4 * out_n), BF16),
        ),
        in_specs=[vmem_spec()] * 3,
        out_specs=(vmem_spec(),) * 3,
        scratch_shapes=[VMEM((half * half + half, 4 * mid_n), F32)],
        compiler_params=pltpu.CompilerParams(vmem_limit_bytes=20 * MIB),
        cost_estimate=pl.CostEstimate(flops=10**9, bytes_accessed=4 * 10**6, transcendentals=0),
    )(cells, w_conv1.reshape(groups * 9 * in1, out1), w_conv2.reshape(groups * 9 * in2, out2))

    message = pl.pallas_call(
        token_kernel,
        name="token",
        out_shape=jax.ShapeDtypeStruct((tokens + 16, out_n), BF16),
        in_specs=[vmem_spec()] * 6,
        out_specs=vmem_spec(),
        scratch_shapes=[
            VMEM((half * half, mid_n), F32),
            VMEM((2 * half, mid_n), F32),
            VMEM((tokens + 2 * quarter, 4 * mid_n), BF16),
            VMEM((tokens + 2 * quarter, 4 * out_n), F32),
            VMEM((out_n // 128, tokens, 128), F32),
        ],
        compiler_params=pltpu.CompilerParams(vmem_limit_bytes=20 * MIB),
    )(facts, partial, prior, second, dense1, dense2)

    far = swapped(message, "heads", 2)
    near = swapped(message, "heads", 1)
    far_near = swapped(far, "heads", 1)

    tile_n = lax.axis_size("tiles")
    latent_n, width = queries.shape
    head_n = width // HEAD_DIM
    share = latent_n // tile_n
    few = tile_n == 4
    part_n = 4
    part_rows = latent_n // part_n
    place = lax.axis_index("tiles") if few else jnp.int32(0)
    place = place.astype(jnp.int32).reshape(1)
    parts = pl.pallas_call(
        attention_kernel,
        name="attention",
        out_shape=(jax.ShapeDtypeStruct((part_rows + 8, width), F32),) * part_n,
        in_specs=[smem_spec()] + [vmem_spec()] * 7,
        out_specs=(vmem_spec(),) * part_n,
        scratch_shapes=[
            VMEM((4 * tokens, width), BF16),
            VMEM((4 * tokens, width), BF16),
            VMEM((latent_n, width), F32),
            VMEM((latent_n, width), F32),
        ],
        compiler_params=pltpu.CompilerParams(vmem_limit_bytes=20 * MIB),
    )(place, message, near, far, far_near, w_key, w_value, queries)

    if few:
        received = [swapped(parts[k], "tiles", k) for k in (3, 2, 1)]
        return pl.pallas_call(
            lambda *refs: merge_kernel(head_n, *refs),
            name="merge",
            out_shape=jax.ShapeDtypeStruct((part_rows, width), BF16),
            in_specs=[vmem_spec()] * 4,
            out_specs=vmem_spec(),
            compiler_params=pltpu.CompilerParams(vmem_limit_bytes=4 * MIB),
        )(parts[0], *received)
    parts = jnp.stack(parts)
    stats = parts[:, part_rows : part_rows + 4]
    stats = stats.transpose(0, 2, 1).reshape(tile_n, share, 4)
    weighted = parts[:, :part_rows].reshape(tile_n, share, width)
    stats = lax.all_to_all(stats, "tiles", 0, 0)
    weighted = lax.all_to_all(weighted, "tiles", 0, 0)
    peaks, totals = stats[..., :head_n], stats[..., head_n : 2 * head_n]
    scale = jnp.exp(peaks - jnp.max(peaks, axis=0, keepdims=True))
    scale = scale / jnp.sum(scale * totals, axis=0, keepdims=True)
    return jnp.sum(weighted * jnp.repeat(scale, HEAD_DIM, axis=2), axis=0).astype(BF16)


def solution(mesh):
    in_specs = (
        P(("slides", "tiles", "heads"), None, None),
        P(),
        P(),
        P(),
        P(None, "heads"),
        P(None, "heads"),
        P(None, "heads"),
        P(("slides", "tiles", "heads")),
        P(("slides", "tiles", "heads")),
        P(("slides", "tiles", "heads"), None),
    )
    out_specs = P(("slides", "tiles"), "heads")
    return jax.shard_map(
        per_device, mesh=mesh, in_specs=in_specs, out_specs=out_specs, check_vma=False
    )
```

```python
import jax
import jax.numpy as jnp
from jax import lax
from jax.experimental import pallas as pl
from jax.experimental.pallas import tpu as pltpu
from jax.sharding import PartitionSpec as P

HEAD_DIM = 64
NEG_BIG = -1e30
LN_EPS = 1e-05
F32 = jnp.float32
BF16 = jnp.bfloat16
VMEM = pltpu.VMEM
SMEM = pltpu.SMEM
MIB = 1 << 20
FIRST_VMEM = 60 * MIB
PACK = 1 << 16


def vmem_spec():
    return pl.BlockSpec(memory_space=VMEM)


def smem_spec():
    return pl.BlockSpec(memory_space=SMEM)


def expand_weights(flat, in_group, out_group, dense_ref):
    groups = flat.shape[0] // (9 * in_group)
    wide = groups * out_group
    source = lax.broadcasted_iota(jnp.int32, (out_group, wide), 0)
    target = lax.broadcasted_iota(jnp.int32, (out_group, wide), 1)
    spread = (lax.rem(target, out_group) == source).astype(BF16)
    tiled = jnp.dot(flat, spread, preferred_element_type=F32)
    row = lax.broadcasted_iota(jnp.int32, tiled.shape, 0)
    lane = lax.broadcasted_iota(jnp.int32, tiled.shape, 1)
    own = lax.div(row, 9 * in_group) == lax.div(lane, out_group)
    tiled = jnp.where(own, tiled, 0.0).astype(BF16)
    dense_ref[...] = jnp.zeros_like(dense_ref)
    for group in range(groups):
        for tap_row in range(3):
            for tap_col in range(3):
                py, px = int(tap_row != 1), int(tap_col != 1)
                block = 2 * int(tap_row == 0) + int(tap_col == 0)
                first = (9 * group + 3 * tap_row + tap_col) * in_group
                to_row = (2 * py + px) * groups * in_group + group * in_group
                dense_ref[pl.ds(to_row, in_group), pl.ds(block * wide, wide)] = tiled[
                    first : first + in_group
                ]


def shifted_down(x):
    row = lax.broadcasted_iota(jnp.int32, x.shape, 0)
    return jnp.where(row == 0, 0.0, pltpu.roll(x, 1, 0))


def normalised(deep):
    deep = jnp.maximum(deep, 0.0)
    centred = deep - jnp.mean(deep, axis=1, keepdims=True)
    spread = jnp.mean(centred * centred, axis=1, keepdims=True)
    return (centred * lax.rsqrt(spread + LN_EPS)).astype(BF16)


def expand_kernel(w1_ref, w2_ref, dense1_ref, dense2_ref):
    expand_weights(w1_ref[...], w1_ref.shape[0] // 36, w1_ref.shape[1], dense1_ref)
    expand_weights(w2_ref[...], w2_ref.shape[0] // 36, w2_ref.shape[1], dense2_ref)


def first_kernel(side, packed_any, adjacency_any, w_any, w1_any, w2_any, pixels_any, token_ref,
                 edge_ref, border_ref, tiny_ref, packed, adjacency, weight, w1, w2, pixels,
                 cells_ref, even_lines, odd_lines, dense1_ref, dense2_ref, wide1, partial, cells,
                 wide2, sems):
    copies = [
        pltpu.make_async_copy(source, target, sems.at[k])
        for k, (source, target) in enumerate((
            (w1_any, w1), (w2_any, w2), (pixels_any, pixels), (w_any, weight),
            (packed_any, packed), (adjacency_any, adjacency),
        ))
    ]
    for copy in copies:
        copy.start()
    copies[0].wait()
    expand_weights(w1[...], w1.shape[0] // 36, w1.shape[1], dense1_ref)
    copies[1].wait()
    expand_weights(w2[...], w2.shape[0] // 36, w2.shape[1], dense2_ref)
    stem_n, half = weight.shape[0], side // 2
    rows, span = 4 * half, 4 * side
    row = lax.broadcasted_iota(jnp.int32, (rows, 2 * span), 0)
    column = lax.broadcasted_iota(jnp.int32, (rows, 2 * span), 1)
    line = 2 * lax.div(lax.rem(row, 2 * half), half) + lax.div(row, 2 * half)
    wanted = line * side + 2 * lax.rem(row, half)
    pick = (lax.rem(column, span) == wanted + lax.div(column, span)).astype(BF16)
    for copy in copies[2:]:
        copy.wait()
    live = (packed[0, 0] >= PACK).astype(F32)
    tissue = lax.rem(packed[0, 0], PACK)
    gates = [(adjacency[0, k] == 0).astype(F32) for k in range(3)]
    row = lax.broadcasted_iota(jnp.int32, (16, cells_ref.shape[1]), 0)
    facts = jnp.zeros(row.shape, F32)
    for k, fact in enumerate([live] + gates + [live * tissue.astype(F32)]):
        facts = jnp.where(row == k, fact, facts)
    cells_ref[pl.ds(half * half, 16)] = facts.astype(BF16)
    border_ref[pl.ds(4 * half, 16)] = facts.astype(BF16)
    flat = jnp.dot(weight[...], pixels[0], preferred_element_type=F32)
    flat = (jnp.maximum(flat, 0.0) * live).astype(BF16)
    blank = jnp.zeros((stem_n, span), BF16)
    for k in range(side // 4):
        four = flat[:, k * span : (k + 1) * span]
        both = jnp.concatenate(
            [jnp.concatenate([four, blank], axis=0), jnp.concatenate([blank, four], axis=0)],
            axis=1,
        )
        sorted_ = lax.dot_general(
            pick, both, (((1,), (1,)), ((), ())), preferred_element_type=F32
        )
        here = pl.ds(k * 2 * half, 2 * half)
        even_lines[here] = sorted_[: 2 * half]
        odd_lines[here] = sorted_[2 * half :]
        cells_ref[here, pl.ds(0, 2 * stem_n)] = sorted_[: 2 * half].astype(BF16)
        cells_ref[here, pl.ds(2 * stem_n, 2 * stem_n)] = sorted_[2 * half :].astype(BF16)
    border_ref[pl.ds(0, 2 * half)] = cells_ref[pl.ds((half - 2) * half, 2 * half)]
    for which in range(2):
        for py, lines in enumerate((even_lines, odd_lines)):
            border_ref[
                pl.ds((2 + which) * half, half), pl.ds(py * 2 * stem_n, 2 * stem_n)
            ] = lines[pl.ds(half - 2 + which, half, stride=half)].astype(BF16)
    tiny_ref[pl.ds(0, 16)] = cells_ref[pl.ds((half - 1) * half - 16, 16)]
    tiny_ref[pl.ds(16, 16)] = cells_ref[pl.ds(half * half - 16, 16)]
    positions, channels = partial.shape
    chunk = 8 * half
    wide1[pl.ds(0, half)] = jnp.zeros((half, wide1.shape[1]), F32)
    row = lax.broadcasted_iota(jnp.int32, (chunk, channels), 0)
    first = lax.rem(row, half) == 0
    dense = dense1_ref[...]
    lane = [pl.ds(b * channels, channels) for b in range(4)]
    for k in range(positions // chunk):
        wide1[pl.ds(half + k * chunk, chunk)] = jnp.dot(
            cells_ref[pl.ds(k * chunk, chunk)], dense, preferred_element_type=F32
        )
        here = pl.ds(half + k * chunk, chunk)
        up = pl.ds(k * chunk, chunk)
        before = wide1[here, lane[1]] + wide1[up, lane[3]]
        before = jnp.where(first, 0.0, pltpu.roll(before, 1, 0))
        partial[pl.ds(k * chunk, chunk)] = wide1[here, lane[0]] + wide1[up, lane[2]] + before
    edge_ref[pl.ds(0, 2 * half)] = partial[pl.ds(0, 2 * half)]
    edge_ref[pl.ds(2 * half, half)] = partial[pl.ds(0, half, stride=half)]
    edge_ref[pl.ds(3 * half, half)] = partial[pl.ds(1, half, stride=half)]
    edge_ref[pl.ds(4 * half, 8)] = facts[0:8, :channels]
    quarter = half // 2
    for i in range(half):
        for px in range(2):
            cells[
                pl.ds((i // 2) * quarter, quarter), pl.ds((2 * (i % 2) + px) * channels, channels)
            ] = jnp.maximum(partial[pl.ds(i * half + px, quarter, stride=2)], 0.0).astype(BF16)
    tokens = quarter * quarter
    out_n = dense2_ref.shape[1] // 4
    block = [pl.ds(b * out_n, out_n) for b in range(4)]
    wide2[pl.ds(0, quarter)] = jnp.zeros((quarter, wide2.shape[1]), F32)
    here, up = pl.ds(quarter, tokens), pl.ds(0, tokens)
    wide2[here] = jnp.dot(cells[...], dense2_ref[...], preferred_element_type=F32)
    before = wide2[here, block[1]] + wide2[up, block[3]]
    row = lax.broadcasted_iota(jnp.int32, before.shape, 0)
    before = jnp.where(lax.rem(row, quarter) == 0, 0.0, pltpu.roll(before, 1, 0))
    deep = wide2[here, block[0]] + wide2[up, block[2]] + before
    token_ref[pl.ds(0, tokens)] = normalised(deep)
    token_ref[pl.ds(tokens, 16)] = cells_ref[pl.ds(positions, 16)]


def rim_kernel(edge_ref, prior_ref, second_ref, dense1_ref, dense2_ref, rim_ref,
               lines, cells):
    half, channels = (edge_ref.shape[0] - 8) // 4, edge_ref.shape[1]
    quarter = half // 2
    facts = edge_ref[pl.ds(4 * half, 8)]
    live, above, beside, corner, known = [facts[k : k + 1, 0:1] for k in range(5)]
    lane = [slice(b * channels, (b + 1) * channels) for b in range(4)]
    dense1 = dense1_ref[...]
    prior = jnp.dot(prior_ref[pl.ds(0, 4 * half)], dense1, preferred_element_type=F32)
    second = jnp.dot(second_ref[...], dense1, preferred_element_type=F32)
    facts = prior_ref[pl.ds(4 * half, 16), pl.ds(0, channels)].astype(F32)
    live_prior, above_prior, beside_prior = facts[0:1], facts[1:2], facts[2:3]
    row_30 = prior[0:half]
    row_31 = prior[half : 2 * half]
    col_30 = prior[2 * half : 3 * half]
    col_31 = prior[3 * half : 4 * half]
    at_zero = lax.broadcasted_iota(jnp.int32, (half, channels), 0) == 0
    top = above * (row_31[:, lane[2]] + shifted_down(row_31[:, lane[3]]))
    top = top + jnp.where(at_zero, corner * row_31[half - 1 : half, lane[3]], 0.0)
    side = beside * (col_31[:, lane[1]] + shifted_down(col_31[:, lane[3]]))
    own = [edge_ref[pl.ds(k * half, half)] for k in range(4)]
    own[0] = own[0] + top + jnp.where(at_zero, side, 0.0)
    own[1] = own[1] + jnp.where(at_zero, side[1:2], 0.0)
    own[2] = own[2] + side + jnp.where(at_zero, top, 0.0)
    own[3] = own[3] + jnp.where(at_zero, top[1:2], 0.0)
    for k in range(4):
        lines[pl.ds(k * half, half)] = jnp.maximum(own[k], 0.0) * live
    over_last, left_last, last = second[15:16], second[30:31], second[31:32]
    row_sum = row_31[:, lane[0]] + row_30[:, lane[2]]
    row_sum = row_sum + shifted_down(row_31[:, lane[1]] + row_30[:, lane[3]])
    row_sum = row_sum + jnp.where(
        at_zero, beside_prior * (last[:, lane[1]] + over_last[:, lane[3]]), 0.0
    )
    col_sum = col_31[:, lane[0]] + col_30[:, lane[1]]
    col_sum = col_sum + shifted_down(col_31[:, lane[2]] + col_30[:, lane[3]])
    col_sum = col_sum + jnp.where(
        at_zero, above_prior * (last[:, lane[2]] + left_last[:, lane[3]]), 0.0
    )
    lines[pl.ds(4 * half, half)] = jnp.maximum(row_sum, 0.0) * live_prior
    lines[pl.ds(5 * half, half)] = jnp.maximum(col_sum, 0.0) * live_prior
    cells[pl.ds(2 * quarter, 2 * quarter)] = jnp.zeros((2 * quarter, cells.shape[1]), BF16)

    def put(which, py, px, line, parity):
        cells[pl.ds(which * quarter, quarter), pl.ds((2 * py + px) * channels, channels)] = lines[
            pl.ds(line * half + parity, quarter, stride=2)
        ].astype(BF16)

    for a in range(2):
        for b in range(2):
            put(0, a, b, a, b)
            put(1, a, b, 2 + b, a)
        put(2, 1, a, 4, a)
        put(3, a, 1, 5, a)
    out_n = dense2_ref.shape[1] // 4
    wide = jnp.dot(cells[...], dense2_ref[...], preferred_element_type=F32)
    part = [
        [wide[k * quarter : (k + 1) * quarter, b * out_n : (b + 1) * out_n] for b in range(4)]
        for k in range(4)
    ]
    row0, col0, over, left = part
    at_zero = lax.broadcasted_iota(jnp.int32, (quarter, out_n), 0) == 0
    deep_row = row0[0] + shifted_down(row0[1]) + above * (over[2] + shifted_down(over[3]))
    deep_row = deep_row + jnp.where(
        at_zero, beside * left[1] + corner * over[3][quarter - 1 : quarter], 0.0
    )
    deep_col = col0[0] + shifted_down(col0[2]) + beside * (left[1] + shifted_down(left[3]))
    rim_ref[pl.ds(0, quarter)] = normalised(deep_row)
    rim_ref[pl.ds(quarter, quarter)] = normalised(deep_col)
    rim_ref[pl.ds(2 * quarter, 16)] = jnp.broadcast_to(known, (16, out_n)).astype(BF16)


def queries_of(place_ref, q_ref, parts, part_n):
    rows = q_ref.shape[0] // part_n
    found = [
        q_ref[pl.ds(pl.multiple_of((place_ref[0] ^ k) * rows, rows), rows)].astype(F32)
        for k in parts
    ]
    return jnp.concatenate(found, axis=0) * (float(HEAD_DIM) ** -0.5)


def by_head(q):
    lane = lax.broadcasted_iota(jnp.int32, q.shape, 1)
    head_n = q.shape[1] // HEAD_DIM
    return jnp.concatenate(
        [jnp.where(lax.div(lane, HEAD_DIM) == h, q, 0.0) for h in range(head_n)], axis=0
    ).astype(BF16)


def softmax_part(q, pieces):
    rows, width = q.shape
    head_n = width // HEAD_DIM
    lane = lax.broadcasted_iota(jnp.int32, (rows, width), 1)
    q = by_head(q)
    scores = [
        lax.dot_general(q, keys, (((1,), (1,)), ((), ())), preferred_element_type=F32) + bias
        for keys, _, bias in pieces
    ]
    peak = jnp.max(scores[0], axis=1, keepdims=True)
    for more in scores[1:]:
        peak = jnp.maximum(peak, jnp.max(more, axis=1, keepdims=True))
    total = summed = 0.0
    for score, (_, values, _) in zip(scores, pieces):
        weights = jnp.exp(score - peak)
        total = total + jnp.sum(weights, axis=1, keepdims=True)
        summed = summed + jnp.dot(weights.astype(BF16), values, preferred_element_type=F32)
    joined = summed[:rows]
    facts = jnp.zeros((rows, width), F32)
    for h in range(head_n):
        mine = slice(h * rows, (h + 1) * rows)
        joined = jnp.where(lax.div(lane, HEAD_DIM) == h, summed[mine], joined)
        facts = jnp.where(lane == h, peak[mine], facts)
        facts = jnp.where(lane == head_n + h, total[mine], facts)
    return joined, facts


def main_kernel(part_n, place_ref, t0, t1, t2, t3, wk_ref, wv_ref, q_ref, sum_ref, facts_ref,
                keys, values, bias_ref):
    tokens = t0.shape[0] - 16
    quarter = int(round(tokens**0.5))
    width = q_ref.shape[1]
    both = jnp.concatenate([wk_ref[...], wv_ref[...]], axis=1)
    masks = []
    spot = lax.broadcasted_iota(jnp.int32, (1, tokens), 1)
    inside = (spot >= quarter) & (lax.rem(spot, quarter) != 0)
    for b, ref in enumerate((t0, t1, t2, t3)):
        made = jnp.dot(ref[pl.ds(0, tokens)], both, preferred_element_type=F32).astype(BF16)
        keys[pl.ds(b * tokens, tokens)] = made[:, :width]
        values[pl.ds(b * tokens, tokens)] = made[:, width:]
        known = ref[pl.ds(tokens, 16), pl.ds(0, tokens)].astype(F32)[4:5]
        masks.append(jnp.where(inside & (spot.astype(F32) < known), 0.0, NEG_BIG))
    bias = jnp.concatenate(masks, axis=1)
    bias_ref[...] = jnp.broadcast_to(bias, bias_ref.shape)
    rows = sum_ref.shape[0] // (part_n - 1)
    pieces = [(keys[...], values[...], bias)]
    for k in range(1, part_n):
        here = pl.ds((k - 1) * rows, rows)
        q = queries_of(place_ref, q_ref, [k], part_n)
        sum_ref[here], facts_ref[here] = softmax_part(q, pieces)


def rest_kernel(part_n, place_ref, t0, t1, t2, t3, wk_ref, wv_ref, q_ref, sum_ref, before_ref,
                keys, values, bias_ref, *out_refs):
    rim = t0.shape[0] - 16
    quarter = rim // 2
    width = q_ref.shape[1]
    head_n = width // HEAD_DIM
    both = jnp.concatenate([wk_ref[...], wv_ref[...]], axis=1)
    spot = lax.broadcasted_iota(jnp.int32, (1, rim), 1)
    token = jnp.where(spot < quarter, spot, (spot - quarter) * quarter)
    masks = []
    for ref in (t0, t1, t2, t3):
        known = ref[pl.ds(rim, 16), pl.ds(0, rim)].astype(F32)[0:1]
        good = (spot != quarter) & (token.astype(F32) < known)
        masks.append(jnp.where(good, 0.0, NEG_BIG))
    bias = jnp.concatenate(masks, axis=1)
    bias_ref[...] = jnp.broadcast_to(bias, bias_ref.shape)
    all_rim = jnp.concatenate([ref[pl.ds(0, rim)] for ref in (t0, t1, t2, t3)], axis=0)
    made = jnp.dot(all_rim, both, preferred_element_type=F32).astype(BF16)
    keys[...] = made[:, :width]
    values[...] = made[:, width:]
    q = queries_of(place_ref, q_ref, range(1, part_n), part_n)
    joined, facts = softmax_part(q, [(made[:, :width], made[:, width:], bias)])
    lane = lax.broadcasted_iota(jnp.int32, facts.shape, 1)
    before = before_ref[...]
    peak = jnp.maximum(facts, before)
    scale_new = jnp.exp(jnp.where(lane < head_n, facts - peak, 0.0))
    scale_old = jnp.exp(jnp.where(lane < head_n, before - peak, 0.0))
    total = facts * pltpu.roll(scale_new, head_n, 1) + before * pltpu.roll(scale_old, head_n, 1)
    wide_new, wide_old = scale_new[:, 0:1], scale_old[:, 0:1]
    for h in range(1, head_n):
        mine = lax.div(lane, HEAD_DIM) == h
        wide_new = jnp.where(mine, scale_new[:, h : h + 1], wide_new)
        wide_old = jnp.where(mine, scale_old[:, h : h + 1], wide_old)
    joined = joined * wide_new + sum_ref[...] * wide_old
    facts = jnp.where(lane < head_n, peak, total)
    rows = q_ref.shape[0] // part_n
    for k, out_ref in enumerate(out_refs):
        out_ref[pl.ds(0, rows)] = joined[k * rows : (k + 1) * rows]
        out_ref[pl.ds(rows, 8)] = facts[k * rows : (k + 1) * rows].T[0:8]


def own_kernel(part_n, place_ref, q_ref, keys, values, bias_ref, rim_keys, rim_values,
               rim_bias_ref, out_ref):
    joined, facts = softmax_part(
        queries_of(place_ref, q_ref, [0], part_n),
        [
            (keys[...], values[...], bias_ref[pl.ds(0, 1)]),
            (rim_keys[...], rim_values[...], rim_bias_ref[pl.ds(0, 1)]),
        ],
    )
    rows = q_ref.shape[0] // part_n
    out_ref[pl.ds(0, rows)] = joined
    out_ref[pl.ds(rows, 8)] = facts.T[0:8]


def merge_kernel(head_n, *refs):
    in_refs, out_ref = refs[:-1], refs[-1]
    part_rows, width = out_ref.shape
    stats = [ref[pl.ds(part_rows, 8)] for ref in in_refs]
    row8 = lax.broadcasted_iota(jnp.int32, stats[0].shape, 0)
    peak = stats[0]
    for s in stats[1:]:
        peak = jnp.maximum(peak, s)
    scales = [jnp.exp(jnp.where(row8 < head_n, s - peak, 0.0)) for s in stats]
    total = scales[0] * pltpu.roll(stats[0], 8 - head_n, 0)
    for c, s in zip(scales[1:], stats[1:]):
        total = total + c * pltpu.roll(s, 8 - head_n, 0)
    total = jnp.where(row8 < head_n, total, 1.0)
    scales = [c / total for c in scales]
    blank = jnp.zeros((part_rows - 8 * len(scales), part_rows), F32)
    turned = jnp.concatenate(scales + [blank], axis=0).T
    lane = lax.broadcasted_iota(jnp.int32, (part_rows, width), 1)
    result = jnp.zeros((part_rows, width), F32)
    for k, ref in enumerate(in_refs):
        scale = turned[:, 8 * k : 8 * k + 1]
        for h in range(1, head_n):
            scale = jnp.where(
                lax.div(lane, HEAD_DIM) == h, turned[:, 8 * k + h : 8 * k + h + 1], scale
            )
        result = result + ref[pl.ds(0, part_rows)] * scale
    out_ref[...] = result.astype(BF16)


def swapped(x, axis, distance):
    return lax.ppermute(x, axis, [(i, i ^ distance) for i in range(lax.axis_size(axis))])


def per_device(
    pixels, w_stem, w_conv1, w_conv2, w_key, w_value, queries, tile_count, tissue, adjacency
):
    slot_n, area, patch = pixels.shape
    assert slot_n == 1
    side = int(round(area**0.5))
    half, quarter = side // 2, side // 4
    channels = w_stem.shape[1]
    groups, _, in1, out1 = w_conv1.shape
    _, _, in2, out2 = w_conv2.shape
    mid_n, out_n = groups * out1, groups * out2
    tokens = quarter * quarter
    border_rows = 4 * half + 16

    w1 = w_conv1.reshape(groups * 9 * in1, out1)
    w2 = w_conv2.reshape(groups * 9 * in2, out2)
    dense_shapes = ((4 * channels, 4 * mid_n), (4 * mid_n, 4 * out_n))
    message, edge, border, tiny = pl.pallas_call(
        lambda *refs: first_kernel(side, *refs),
        name="first",
        out_shape=(
            jax.ShapeDtypeStruct((tokens + 16, out_n), BF16),
            jax.ShapeDtypeStruct((4 * half + 8, mid_n), F32),
            jax.ShapeDtypeStruct((border_rows, 4 * channels), BF16),
            jax.ShapeDtypeStruct((32, 4 * channels), BF16),
        ),
        in_specs=[pl.BlockSpec(memory_space=pl.ANY)] * 6,
        out_specs=(vmem_spec(),) * 4,
        scratch_shapes=[
            SMEM((1, 1), jnp.int32),
            SMEM((1, 3), jnp.int32),
            VMEM((channels, patch), BF16),
            VMEM(w1.shape, BF16),
            VMEM(w2.shape, BF16),
            VMEM((1, patch, area), BF16),
            VMEM((half * half + 16, 4 * channels), BF16),
            VMEM((half * half, 2 * channels), F32),
            VMEM((half * half, 2 * channels), F32),
            VMEM(dense_shapes[0], BF16),
            VMEM(dense_shapes[1], BF16),
            VMEM((half * half + half, 4 * mid_n), F32),
            VMEM((half * half, mid_n), F32),
            VMEM((tokens, 4 * mid_n), BF16),
            VMEM((tokens + quarter, 4 * out_n), F32),
            pltpu.SemaphoreType.DMA((6,)),
        ],
        compiler_params=pltpu.CompilerParams(vmem_limit_bytes=FIRST_VMEM),
    )(
        (tile_count * PACK + tissue).reshape(1, 1), adjacency, w_stem.T, w1, w2,
        jnp.swapaxes(pixels, 1, 2),
    )

    line = ("tiles", "heads")
    line_n = lax.axis_size("tiles") * lax.axis_size("heads")
    prior = lax.ppermute(border, line, [(i, i + 1) for i in range(line_n - 1)])
    second = lax.ppermute(tiny, line, [(i, i + 2) for i in range(line_n - 2)])
    message, w1, w2 = lax.optimization_barrier((message, w1, w2))
    dense1, dense2 = pl.pallas_call(
        expand_kernel,
        name="expand",
        out_shape=tuple(jax.ShapeDtypeStruct(shape, BF16) for shape in dense_shapes),
        in_specs=[vmem_spec()] * 2,
        out_specs=(vmem_spec(),) * 2,
        compiler_params=pltpu.CompilerParams(vmem_limit_bytes=8 * MIB),
        cost_estimate=pl.CostEstimate(flops=10**9, bytes_accessed=4 * 10**6, transcendentals=0),
    )(w1, w2)
    message, dense1 = lax.optimization_barrier((message, dense1))
    far = swapped(message, "heads", 2)
    near = swapped(message, "heads", 1)
    far_near = swapped(far, "heads", 1)

    rim = pl.pallas_call(
        rim_kernel,
        name="rim",
        out_shape=jax.ShapeDtypeStruct((2 * quarter + 16, out_n), BF16),
        in_specs=[vmem_spec()] * 5,
        out_specs=vmem_spec(),
        scratch_shapes=[
            VMEM((6 * half, mid_n), F32),
            VMEM((4 * quarter, 4 * mid_n), BF16),
        ],
        compiler_params=pltpu.CompilerParams(vmem_limit_bytes=12 * MIB),
        cost_estimate=pl.CostEstimate(flops=20*10**9, bytes_accessed=4 * 10**7, transcendentals=0),
    )(edge, prior, second, dense1, dense2)
    rims = [swapped(rim, "heads", k) for k in (2, 1, 3)]

    tile_n = lax.axis_size("tiles")
    latent_n, width = queries.shape
    head_n = width // HEAD_DIM
    share = latent_n // tile_n
    few = tile_n == 4
    part_n = 4
    part_rows = latent_n // part_n
    place = lax.axis_index("tiles") if few else jnp.int32(0)
    place = place.astype(jnp.int32).reshape(1)
    others = (part_n - 1) * part_rows
    main = pl.pallas_call(
        lambda *refs: main_kernel(part_n, *refs),
        name="main",
        out_shape=(
            jax.ShapeDtypeStruct((others, width), F32),
            jax.ShapeDtypeStruct((others, width), F32),
            jax.ShapeDtypeStruct((4 * tokens, width), BF16),
            jax.ShapeDtypeStruct((4 * tokens, width), BF16),
            jax.ShapeDtypeStruct((8, 4 * tokens), F32),
        ),
        in_specs=[smem_spec()] + [vmem_spec()] * 7,
        out_specs=(vmem_spec(),) * 5,
        compiler_params=pltpu.CompilerParams(vmem_limit_bytes=16 * MIB),
        cost_estimate=pl.CostEstimate(flops=10**6, bytes_accessed=10**4, transcendentals=0),
    )(place, message, near, far, far_near, w_key, w_value, queries)
    rest = pl.pallas_call(
        lambda *refs: rest_kernel(part_n, *refs),
        name="rest",
        out_shape=(
            jax.ShapeDtypeStruct((8 * quarter, width), BF16),
            jax.ShapeDtypeStruct((8 * quarter, width), BF16),
            jax.ShapeDtypeStruct((8, 8 * quarter), F32),
        ) + (jax.ShapeDtypeStruct((part_rows + 8, width), F32),) * (part_n - 1),
        in_specs=[smem_spec()] + [vmem_spec()] * 9,
        out_specs=(vmem_spec(),) * (part_n + 2),
        compiler_params=pltpu.CompilerParams(vmem_limit_bytes=12 * MIB),
        cost_estimate=pl.CostEstimate(
            flops=20 * 10**9, bytes_accessed=4 * 10**7, transcendentals=0
        ),
    )(place, rim, *rims, w_key, w_value, queries, main[0], main[1])
    own = pl.pallas_call(
        lambda *refs: own_kernel(part_n, *refs),
        name="own",
        out_shape=jax.ShapeDtypeStruct((part_rows + 8, width), F32),
        in_specs=[smem_spec()] + [vmem_spec()] * 7,
        out_specs=vmem_spec(),
        compiler_params=pltpu.CompilerParams(vmem_limit_bytes=12 * MIB),
        cost_estimate=pl.CostEstimate(flops=10**9, bytes_accessed=4 * 10**6, transcendentals=0),
    )(place, queries, main[2], main[3], main[4], rest[0], rest[1], rest[2])
    parts = (own,) + tuple(rest[3:])

    if few:
        received = [swapped(parts[k], "tiles", k) for k in (3, 2, 1)]
        return pl.pallas_call(
            lambda *refs: merge_kernel(head_n, *refs),
            name="merge",
            out_shape=jax.ShapeDtypeStruct((part_rows, width), BF16),
            in_specs=[vmem_spec()] * 4,
            out_specs=vmem_spec(),
            compiler_params=pltpu.CompilerParams(vmem_limit_bytes=4 * MIB),
        )(parts[0], *received)
    parts = jnp.stack(parts)
    stats = parts[:, part_rows : part_rows + 4]
    stats = stats.transpose(0, 2, 1).reshape(tile_n, share, 4)
    weighted = parts[:, :part_rows].reshape(tile_n, share, width)
    stats = lax.all_to_all(stats, "tiles", 0, 0)
    weighted = lax.all_to_all(weighted, "tiles", 0, 0)
    peaks, totals = stats[..., :head_n], stats[..., head_n : 2 * head_n]
    scale = jnp.exp(peaks - jnp.max(peaks, axis=0, keepdims=True))
    scale = scale / jnp.sum(scale * totals, axis=0, keepdims=True)
    return jnp.sum(weighted * jnp.repeat(scale, HEAD_DIM, axis=2), axis=0).astype(BF16)


def solution(mesh):
    in_specs = (
        P(("slides", "tiles", "heads"), None, None),
        P(),
        P(),
        P(),
        P(None, "heads"),
        P(None, "heads"),
        P(None, "heads"),
        P(("slides", "tiles", "heads")),
        P(("slides", "tiles", "heads")),
        P(("slides", "tiles", "heads"), None),
    )
    out_specs = P(("slides", "tiles"), "heads")
    return jax.shard_map(
        per_device, mesh=mesh, in_specs=in_specs, out_specs=out_specs, check_vma=False
    )
```

```python
import jax
import jax.numpy as jnp
from jax import lax
from jax.experimental import pallas as pl
from jax.experimental.pallas import tpu as pltpu
from jax.sharding import PartitionSpec as P

HEAD_DIM = 64
NEG_BIG = -1e30
LN_EPS = 1e-05
F32 = jnp.float32
BF16 = jnp.bfloat16
VMEM = pltpu.VMEM
SMEM = pltpu.SMEM
MIB = 1 << 20
FIRST_VMEM = 60 * MIB
PACK = 1 << 16
ORDER = (3, 0, 2, 1)


def vmem_spec():
    return pl.BlockSpec(memory_space=VMEM)


def smem_spec():
    return pl.BlockSpec(memory_space=SMEM)


def wide_dots(cells, dense_ref):
    part, out_n = dense_ref.shape[0] // 4, dense_ref.shape[1] // 4
    return [
        jnp.dot(
            cells[:, first * part : last * part],
            dense_ref[pl.ds(first * part, (last - first) * part), pl.ds(b * out_n, out_n)],
            preferred_element_type=F32,
        )
        for b, (first, last) in enumerate(((0, 4), (0, 2), (1, 3), (1, 2)))
    ]


def expand_weights(flat, in_group, out_group, dense_ref, order=(0, 1, 2, 3)):
    groups = flat.shape[0] // (9 * in_group)
    wide = groups * out_group
    source = lax.broadcasted_iota(jnp.int32, (out_group, wide), 0)
    target = lax.broadcasted_iota(jnp.int32, (out_group, wide), 1)
    spread = (lax.rem(target, out_group) == source).astype(BF16)
    tiled = jnp.dot(flat, spread, preferred_element_type=F32)
    row = lax.broadcasted_iota(jnp.int32, tiled.shape, 0)
    lane = lax.broadcasted_iota(jnp.int32, tiled.shape, 1)
    own = lax.div(row, 9 * in_group) == lax.div(lane, out_group)
    tiled = jnp.where(own, tiled, 0.0).astype(BF16)
    dense_ref[...] = jnp.zeros_like(dense_ref)
    for group in range(groups):
        for tap_row in range(3):
            for tap_col in range(3):
                py, px = int(tap_row != 1), int(tap_col != 1)
                block = 2 * int(tap_row == 0) + int(tap_col == 0)
                first = (9 * group + 3 * tap_row + tap_col) * in_group
                to_row = order[2 * py + px] * groups * in_group + group * in_group
                dense_ref[pl.ds(to_row, in_group), pl.ds(block * wide, wide)] = tiled[
                    first : first + in_group
                ]


def shifted_down(x):
    row = lax.broadcasted_iota(jnp.int32, x.shape, 0)
    return jnp.where(row == 0, 0.0, pltpu.roll(x, 1, 0))


def normalised(deep):
    deep = jnp.maximum(deep, 0.0)
    centred = deep - jnp.mean(deep, axis=1, keepdims=True)
    spread = jnp.mean(centred * centred, axis=1, keepdims=True)
    return (centred * lax.rsqrt(spread + LN_EPS)).astype(BF16)


def expand_kernel(w1_ref, w2_ref, dense1_ref, dense2_ref):
    expand_weights(w1_ref[...], w1_ref.shape[0] // 36, w1_ref.shape[1], dense1_ref)
    expand_weights(w2_ref[...], w2_ref.shape[0] // 36, w2_ref.shape[1], dense2_ref, ORDER)


def first_kernel(side, packed_any, adjacency_any, w_any, w1_any, w2_any, pixels_any, token_ref,
                 edge_ref, border_ref, tiny_ref, packed, adjacency, weight, w1, w2, pixels,
                 cells_ref, even_lines, odd_lines, dense1_ref, dense2_ref, wide1, partial, cells,
                 wide2, sems):
    copies = [
        pltpu.make_async_copy(source, target, sems.at[k])
        for k, (source, target) in enumerate((
            (w1_any, w1), (w2_any, w2), (pixels_any, pixels), (w_any, weight),
            (packed_any, packed), (adjacency_any, adjacency),
        ))
    ]
    for copy in copies:
        copy.start()
    copies[0].wait()
    expand_weights(w1[...], w1.shape[0] // 36, w1.shape[1], dense1_ref)
    copies[1].wait()
    expand_weights(w2[...], w2.shape[0] // 36, w2.shape[1], dense2_ref, ORDER)
    stem_n, half = weight.shape[0], side // 2
    rows, span = 4 * half, 4 * side
    row = lax.broadcasted_iota(jnp.int32, (rows, 2 * span), 0)
    column = lax.broadcasted_iota(jnp.int32, (rows, 2 * span), 1)
    line = 2 * lax.div(lax.rem(row, 2 * half), half) + lax.div(row, 2 * half)
    wanted = line * side + 2 * lax.rem(row, half)
    pick = (lax.rem(column, span) == wanted + lax.div(column, span)).astype(BF16)
    for copy in copies[2:]:
        copy.wait()
    live = (packed[0, 0] >= PACK).astype(F32)
    tissue = lax.rem(packed[0, 0], PACK)
    gates = [(adjacency[0, k] == 0).astype(F32) for k in range(3)]
    row = lax.broadcasted_iota(jnp.int32, (16, cells_ref.shape[1]), 0)
    facts = jnp.zeros(row.shape, F32)
    for k, fact in enumerate([live] + gates + [live * tissue.astype(F32)]):
        facts = jnp.where(row == k, fact, facts)
    cells_ref[pl.ds(half * half, 16)] = facts.astype(BF16)
    border_ref[pl.ds(4 * half, 16)] = facts.astype(BF16)
    flat = jnp.dot(weight[...], pixels[0], preferred_element_type=F32)
    flat = (jnp.maximum(flat, 0.0) * live).astype(BF16)
    blank = jnp.zeros((stem_n, span), BF16)
    for k in range(side // 4):
        four = flat[:, k * span : (k + 1) * span]
        both = jnp.concatenate(
            [jnp.concatenate([four, blank], axis=0), jnp.concatenate([blank, four], axis=0)],
            axis=1,
        )
        sorted_ = lax.dot_general(
            pick, both, (((1,), (1,)), ((), ())), preferred_element_type=F32
        )
        here = pl.ds(k * 2 * half, 2 * half)
        even_lines[here] = sorted_[: 2 * half]
        odd_lines[here] = sorted_[2 * half :]
        cells_ref[here, pl.ds(0, 2 * stem_n)] = sorted_[: 2 * half].astype(BF16)
        cells_ref[here, pl.ds(2 * stem_n, 2 * stem_n)] = sorted_[2 * half :].astype(BF16)
    border_ref[pl.ds(0, 2 * half)] = cells_ref[pl.ds((half - 2) * half, 2 * half)]
    for which in range(2):
        for py, lines in enumerate((even_lines, odd_lines)):
            border_ref[
                pl.ds((2 + which) * half, half), pl.ds(py * 2 * stem_n, 2 * stem_n)
            ] = lines[pl.ds(half - 2 + which, half, stride=half)].astype(BF16)
    tiny_ref[pl.ds(0, 16)] = cells_ref[pl.ds((half - 1) * half - 16, 16)]
    tiny_ref[pl.ds(16, 16)] = cells_ref[pl.ds(half * half - 16, 16)]
    positions, channels = partial.shape
    chunk = 8 * half
    wide1[pl.ds(0, half)] = jnp.zeros((half, wide1.shape[1]), F32)
    row = lax.broadcasted_iota(jnp.int32, (chunk, channels), 0)
    first = lax.rem(row, half) == 0
    dense = dense1_ref[...]
    lane = [pl.ds(b * channels, channels) for b in range(4)]
    for k in range(positions // chunk):
        wide1[pl.ds(half + k * chunk, chunk)] = jnp.dot(
            cells_ref[pl.ds(k * chunk, chunk)], dense, preferred_element_type=F32
        )
        here = pl.ds(half + k * chunk, chunk)
        up = pl.ds(k * chunk, chunk)
        before = wide1[here, lane[1]] + wide1[up, lane[3]]
        before = jnp.where(first, 0.0, pltpu.roll(before, 1, 0))
        partial[pl.ds(k * chunk, chunk)] = wide1[here, lane[0]] + wide1[up, lane[2]] + before
    edge_ref[pl.ds(0, 2 * half)] = partial[pl.ds(0, 2 * half)]
    edge_ref[pl.ds(2 * half, half)] = partial[pl.ds(0, half, stride=half)]
    edge_ref[pl.ds(3 * half, half)] = partial[pl.ds(1, half, stride=half)]
    edge_ref[pl.ds(4 * half, 8)] = facts[0:8, :channels]
    quarter = half // 2
    for i in range(half):
        for px in range(2):
            cells[
                pl.ds((i // 2) * quarter, quarter),
                pl.ds(ORDER[2 * (i % 2) + px] * channels, channels),
            ] = jnp.maximum(partial[pl.ds(i * half + px, quarter, stride=2)], 0.0).astype(BF16)
    tokens = quarter * quarter
    out_n = dense2_ref.shape[1] // 4
    block = [pl.ds(b * out_n, out_n) for b in range(4)]
    wide2[pl.ds(0, quarter)] = jnp.zeros((quarter, wide2.shape[1]), F32)
    here, up = pl.ds(quarter, tokens), pl.ds(0, tokens)
    for b, product in enumerate(wide_dots(cells[...], dense2_ref)):
        wide2[here, block[b]] = product
    before = wide2[here, block[1]] + wide2[up, block[3]]
    row = lax.broadcasted_iota(jnp.int32, before.shape, 0)
    before = jnp.where(lax.rem(row, quarter) == 0, 0.0, pltpu.roll(before, 1, 0))
    deep = wide2[here, block[0]] + wide2[up, block[2]] + before
    token_ref[pl.ds(0, tokens)] = normalised(deep)
    token_ref[pl.ds(tokens, 16)] = cells_ref[pl.ds(positions, 16)]


def rim_kernel(edge_ref, prior_ref, second_ref, dense1_ref, dense2_ref, rim_ref,
               lines, cells):
    half, channels = (edge_ref.shape[0] - 8) // 4, edge_ref.shape[1]
    quarter = half // 2
    facts = edge_ref[pl.ds(4 * half, 8)]
    live, above, beside, corner, known = [facts[k : k + 1, 0:1] for k in range(5)]
    lane = [slice(b * channels, (b + 1) * channels) for b in range(4)]
    dense1 = dense1_ref[...]
    prior = jnp.dot(prior_ref[pl.ds(0, 4 * half)], dense1, preferred_element_type=F32)
    second = jnp.dot(second_ref[...], dense1, preferred_element_type=F32)
    facts = prior_ref[pl.ds(4 * half, 16), pl.ds(0, channels)].astype(F32)
    live_prior, above_prior, beside_prior = facts[0:1], facts[1:2], facts[2:3]
    row_30 = prior[0:half]
    row_31 = prior[half : 2 * half]
    col_30 = prior[2 * half : 3 * half]
    col_31 = prior[3 * half : 4 * half]
    at_zero = lax.broadcasted_iota(jnp.int32, (half, channels), 0) == 0
    top = above * (row_31[:, lane[2]] + shifted_down(row_31[:, lane[3]]))
    top = top + jnp.where(at_zero, corner * row_31[half - 1 : half, lane[3]], 0.0)
    side = beside * (col_31[:, lane[1]] + shifted_down(col_31[:, lane[3]]))
    own = [edge_ref[pl.ds(k * half, half)] for k in range(4)]
    own[0] = own[0] + top + jnp.where(at_zero, side, 0.0)
    own[1] = own[1] + jnp.where(at_zero, side[1:2], 0.0)
    own[2] = own[2] + side + jnp.where(at_zero, top, 0.0)
    own[3] = own[3] + jnp.where(at_zero, top[1:2], 0.0)
    for k in range(4):
        lines[pl.ds(k * half, half)] = jnp.maximum(own[k], 0.0) * live
    over_last, left_last, last = second[15:16], second[30:31], second[31:32]
    row_sum = row_31[:, lane[0]] + row_30[:, lane[2]]
    row_sum = row_sum + shifted_down(row_31[:, lane[1]] + row_30[:, lane[3]])
    row_sum = row_sum + jnp.where(
        at_zero, beside_prior * (last[:, lane[1]] + over_last[:, lane[3]]), 0.0
    )
    col_sum = col_31[:, lane[0]] + col_30[:, lane[1]]
    col_sum = col_sum + shifted_down(col_31[:, lane[2]] + col_30[:, lane[3]])
    col_sum = col_sum + jnp.where(
        at_zero, above_prior * (last[:, lane[2]] + left_last[:, lane[3]]), 0.0
    )
    lines[pl.ds(4 * half, half)] = jnp.maximum(row_sum, 0.0) * live_prior
    lines[pl.ds(5 * half, half)] = jnp.maximum(col_sum, 0.0) * live_prior
    cells[pl.ds(2 * quarter, 2 * quarter)] = jnp.zeros((2 * quarter, cells.shape[1]), BF16)

    def put(which, py, px, line, parity):
        cells[pl.ds(which * quarter, quarter), pl.ds(ORDER[2 * py + px] * channels, channels)] = lines[
            pl.ds(line * half + parity, quarter, stride=2)
        ].astype(BF16)

    for a in range(2):
        for b in range(2):
            put(0, a, b, a, b)
            put(1, a, b, 2 + b, a)
        put(2, 1, a, 4, a)
        put(3, a, 1, 5, a)
    out_n = dense2_ref.shape[1] // 4
    wide = wide_dots(cells[...], dense2_ref)
    part = [[wide[b][k * quarter : (k + 1) * quarter] for b in range(4)] for k in range(4)]
    row0, col0, over, left = part
    at_zero = lax.broadcasted_iota(jnp.int32, (quarter, out_n), 0) == 0
    deep_row = row0[0] + shifted_down(row0[1]) + above * (over[2] + shifted_down(over[3]))
    deep_row = deep_row + jnp.where(
        at_zero, beside * left[1] + corner * over[3][quarter - 1 : quarter], 0.0
    )
    deep_col = col0[0] + shifted_down(col0[2]) + beside * (left[1] + shifted_down(left[3]))
    rim_ref[pl.ds(0, quarter)] = normalised(deep_row)
    rim_ref[pl.ds(quarter, quarter)] = normalised(deep_col)
    rim_ref[pl.ds(2 * quarter, 16)] = jnp.broadcast_to(known, (16, out_n)).astype(BF16)


def queries_of(place_ref, q_ref, parts, part_n):
    rows = q_ref.shape[0] // part_n
    found = [
        q_ref[pl.ds(pl.multiple_of((place_ref[0] ^ k) * rows, rows), rows)].astype(F32)
        for k in parts
    ]
    return jnp.concatenate(found, axis=0) * (float(HEAD_DIM) ** -0.5)


def by_head(q):
    lane = lax.broadcasted_iota(jnp.int32, q.shape, 1)
    head_n = q.shape[1] // HEAD_DIM
    return jnp.concatenate(
        [jnp.where(lax.div(lane, HEAD_DIM) == h, q, 0.0) for h in range(head_n)], axis=0
    ).astype(BF16)


def softmax_part(q, pieces):
    rows, width = q.shape
    head_n = width // HEAD_DIM
    lane = lax.broadcasted_iota(jnp.int32, (rows, width), 1)
    q = by_head(q)
    scores = [
        lax.dot_general(q, keys, (((1,), (1,)), ((), ())), preferred_element_type=F32) + bias
        for keys, _, bias in pieces
    ]
    peak = jnp.max(scores[0], axis=1, keepdims=True)
    for more in scores[1:]:
        peak = jnp.maximum(peak, jnp.max(more, axis=1, keepdims=True))
    total = summed = 0.0
    for score, (_, values, _) in zip(scores, pieces):
        weights = jnp.exp(score - peak)
        total = total + jnp.sum(weights, axis=1, keepdims=True)
        summed = summed + jnp.dot(weights.astype(BF16), values, preferred_element_type=F32)
    joined = summed[:rows]
    facts = jnp.zeros((rows, width), F32)
    for h in range(head_n):
        mine = slice(h * rows, (h + 1) * rows)
        joined = jnp.where(lax.div(lane, HEAD_DIM) == h, summed[mine], joined)
        facts = jnp.where(lane == h, peak[mine], facts)
        facts = jnp.where(lane == head_n + h, total[mine], facts)
    return joined, facts


def main_kernel(part_n, place_ref, t0, t1, t2, t3, wk_ref, wv_ref, q_ref, sum_ref, facts_ref,
                keys, values, bias_ref):
    tokens = t0.shape[0] - 16
    quarter = int(round(tokens**0.5))
    width = q_ref.shape[1]
    both = jnp.concatenate([wk_ref[...], wv_ref[...]], axis=1)
    masks = []
    spot = lax.broadcasted_iota(jnp.int32, (1, tokens), 1)
    inside = (spot >= quarter) & (lax.rem(spot, quarter) != 0)
    for b, ref in enumerate((t0, t1, t2, t3)):
        made = jnp.dot(ref[pl.ds(0, tokens)], both, preferred_element_type=F32).astype(BF16)
        keys[pl.ds(b * tokens, tokens)] = made[:, :width]
        values[pl.ds(b * tokens, tokens)] = made[:, width:]
        known = ref[pl.ds(tokens, 16), pl.ds(0, tokens)].astype(F32)[4:5]
        masks.append(jnp.where(inside & (spot.astype(F32) < known), 0.0, NEG_BIG))
    bias = jnp.concatenate(masks, axis=1)
    bias_ref[...] = jnp.broadcast_to(bias, bias_ref.shape)
    rows = sum_ref.shape[0] // (part_n - 1)
    pieces = [(keys[...], values[...], bias)]
    for k in range(1, part_n):
        here = pl.ds((k - 1) * rows, rows)
        q = queries_of(place_ref, q_ref, [k], part_n)
        sum_ref[here], facts_ref[here] = softmax_part(q, pieces)


def rest_kernel(part_n, place_ref, t0, t1, t2, t3, wk_ref, wv_ref, q_ref, sum_ref, before_ref,
                keys, values, bias_ref, *out_refs):
    rim = t0.shape[0] - 16
    quarter = rim // 2
    width = q_ref.shape[1]
    head_n = width // HEAD_DIM
    both = jnp.concatenate([wk_ref[...], wv_ref[...]], axis=1)
    spot = lax.broadcasted_iota(jnp.int32, (1, rim), 1)
    token = jnp.where(spot < quarter, spot, (spot - quarter) * quarter)
    masks = []
    for ref in (t0, t1, t2, t3):
        known = ref[pl.ds(rim, 16), pl.ds(0, rim)].astype(F32)[0:1]
        good = (spot != quarter) & (token.astype(F32) < known)
        masks.append(jnp.where(good, 0.0, NEG_BIG))
    bias = jnp.concatenate(masks, axis=1)
    bias_ref[...] = jnp.broadcast_to(bias, bias_ref.shape)
    all_rim = jnp.concatenate([ref[pl.ds(0, rim)] for ref in (t0, t1, t2, t3)], axis=0)
    made = jnp.dot(all_rim, both, preferred_element_type=F32).astype(BF16)
    keys[...] = made[:, :width]
    values[...] = made[:, width:]
    q = queries_of(place_ref, q_ref, range(1, part_n), part_n)
    joined, facts = softmax_part(q, [(made[:, :width], made[:, width:], bias)])
    lane = lax.broadcasted_iota(jnp.int32, facts.shape, 1)
    before = before_ref[...]
    peak = jnp.maximum(facts, before)
    scale_new = jnp.exp(jnp.where(lane < head_n, facts - peak, 0.0))
    scale_old = jnp.exp(jnp.where(lane < head_n, before - peak, 0.0))
    total = facts * pltpu.roll(scale_new, head_n, 1) + before * pltpu.roll(scale_old, head_n, 1)
    wide_new, wide_old = scale_new[:, 0:1], scale_old[:, 0:1]
    for h in range(1, head_n):
        mine = lax.div(lane, HEAD_DIM) == h
        wide_new = jnp.where(mine, scale_new[:, h : h + 1], wide_new)
        wide_old = jnp.where(mine, scale_old[:, h : h + 1], wide_old)
    joined = joined * wide_new + sum_ref[...] * wide_old
    facts = jnp.where(lane < head_n, peak, total)
    rows = q_ref.shape[0] // part_n
    for k, out_ref in enumerate(out_refs):
        out_ref[pl.ds(0, rows)] = joined[k * rows : (k + 1) * rows]
        out_ref[pl.ds(rows, 8)] = facts[k * rows : (k + 1) * rows].T[0:8]


def own_kernel(part_n, place_ref, q_ref, keys, values, bias_ref, rim_keys, rim_values,
               rim_bias_ref, out_ref):
    joined, facts = softmax_part(
        queries_of(place_ref, q_ref, [0], part_n),
        [
            (keys[...], values[...], bias_ref[pl.ds(0, 1)]),
            (rim_keys[...], rim_values[...], rim_bias_ref[pl.ds(0, 1)]),
        ],
    )
    rows = q_ref.shape[0] // part_n
    out_ref[pl.ds(0, rows)] = joined
    out_ref[pl.ds(rows, 8)] = facts.T[0:8]


def merge_kernel(head_n, *refs):
    in_refs, out_ref = refs[:-1], refs[-1]
    part_rows, width = out_ref.shape
    stats = [ref[pl.ds(part_rows, 8)] for ref in in_refs]
    row8 = lax.broadcasted_iota(jnp.int32, stats[0].shape, 0)
    peak = stats[0]
    for s in stats[1:]:
        peak = jnp.maximum(peak, s)
    scales = [jnp.exp(jnp.where(row8 < head_n, s - peak, 0.0)) for s in stats]
    total = scales[0] * pltpu.roll(stats[0], 8 - head_n, 0)
    for c, s in zip(scales[1:], stats[1:]):
        total = total + c * pltpu.roll(s, 8 - head_n, 0)
    total = jnp.where(row8 < head_n, total, 1.0)
    scales = [c / total for c in scales]
    blank = jnp.zeros((part_rows - 8 * len(scales), part_rows), F32)
    turned = jnp.concatenate(scales + [blank], axis=0).T
    lane = lax.broadcasted_iota(jnp.int32, (part_rows, width), 1)
    result = jnp.zeros((part_rows, width), F32)
    for k, ref in enumerate(in_refs):
        scale = turned[:, 8 * k : 8 * k + 1]
        for h in range(1, head_n):
            scale = jnp.where(
                lax.div(lane, HEAD_DIM) == h, turned[:, 8 * k + h : 8 * k + h + 1], scale
            )
        result = result + ref[pl.ds(0, part_rows)] * scale
    out_ref[...] = result.astype(BF16)


def swapped(x, axis, distance):
    return lax.ppermute(x, axis, [(i, i ^ distance) for i in range(lax.axis_size(axis))])


def per_device(
    pixels, w_stem, w_conv1, w_conv2, w_key, w_value, queries, tile_count, tissue, adjacency
):
    slot_n, area, patch = pixels.shape
    assert slot_n == 1
    side = int(round(area**0.5))
    half, quarter = side // 2, side // 4
    channels = w_stem.shape[1]
    groups, _, in1, out1 = w_conv1.shape
    _, _, in2, out2 = w_conv2.shape
    mid_n, out_n = groups * out1, groups * out2
    tokens = quarter * quarter
    border_rows = 4 * half + 16

    w1 = w_conv1.reshape(groups * 9 * in1, out1)
    w2 = w_conv2.reshape(groups * 9 * in2, out2)
    dense_shapes = ((4 * channels, 4 * mid_n), (4 * mid_n, 4 * out_n))
    message, edge, border, tiny = pl.pallas_call(
        lambda *refs: first_kernel(side, *refs),
        name="first",
        out_shape=(
            jax.ShapeDtypeStruct((tokens + 16, out_n), BF16),
            jax.ShapeDtypeStruct((4 * half + 8, mid_n), F32),
            jax.ShapeDtypeStruct((border_rows, 4 * channels), BF16),
            jax.ShapeDtypeStruct((32, 4 * channels), BF16),
        ),
        in_specs=[pl.BlockSpec(memory_space=pl.ANY)] * 6,
        out_specs=(vmem_spec(),) * 4,
        scratch_shapes=[
            SMEM((1, 1), jnp.int32),
            SMEM((1, 3), jnp.int32),
            VMEM((channels, patch), BF16),
            VMEM(w1.shape, BF16),
            VMEM(w2.shape, BF16),
            VMEM((1, patch, area), BF16),
            VMEM((half * half + 16, 4 * channels), BF16),
            VMEM((half * half, 2 * channels), F32),
            VMEM((half * half, 2 * channels), F32),
            VMEM(dense_shapes[0], BF16),
            VMEM(dense_shapes[1], BF16),
            VMEM((half * half + half, 4 * mid_n), F32),
            VMEM((half * half, mid_n), F32),
            VMEM((tokens, 4 * mid_n), BF16),
            VMEM((tokens + quarter, 4 * out_n), F32),
            pltpu.SemaphoreType.DMA((6,)),
        ],
        compiler_params=pltpu.CompilerParams(vmem_limit_bytes=FIRST_VMEM),
    )(
        (tile_count * PACK + tissue).reshape(1, 1), adjacency, w_stem.T, w1, w2,
        jnp.swapaxes(pixels, 1, 2),
    )

    line = ("tiles", "heads")
    line_n = lax.axis_size("tiles") * lax.axis_size("heads")
    prior = lax.ppermute(border, line, [(i, i + 1) for i in range(line_n - 1)])
    second = lax.ppermute(tiny, line, [(i, i + 2) for i in range(line_n - 2)])
    message, w1, w2 = lax.optimization_barrier((message, w1, w2))
    dense1, dense2 = pl.pallas_call(
        expand_kernel,
        name="expand",
        out_shape=tuple(jax.ShapeDtypeStruct(shape, BF16) for shape in dense_shapes),
        in_specs=[vmem_spec()] * 2,
        out_specs=(vmem_spec(),) * 2,
        compiler_params=pltpu.CompilerParams(vmem_limit_bytes=8 * MIB),
        cost_estimate=pl.CostEstimate(flops=10**9, bytes_accessed=4 * 10**6, transcendentals=0),
    )(w1, w2)
    far = swapped(message, "heads", 2)
    message_n, dense1, prior = lax.optimization_barrier((message, dense1, prior))
    near = swapped(message_n, "heads", 1)
    far_near = swapped(far, "heads", 1)

    rim = pl.pallas_call(
        rim_kernel,
        name="rim",
        out_shape=jax.ShapeDtypeStruct((2 * quarter + 16, out_n), BF16),
        in_specs=[vmem_spec()] * 5,
        out_specs=vmem_spec(),
        scratch_shapes=[
            VMEM((6 * half, mid_n), F32),
            VMEM((4 * quarter, 4 * mid_n), BF16),
        ],
        compiler_params=pltpu.CompilerParams(vmem_limit_bytes=12 * MIB),
        cost_estimate=pl.CostEstimate(flops=20*10**9, bytes_accessed=4 * 10**7, transcendentals=0),
    )(edge, prior, second, dense1, dense2)
    rims = [swapped(rim, "heads", k) for k in (2, 1, 3)]

    tile_n = lax.axis_size("tiles")
    latent_n, width = queries.shape
    head_n = width // HEAD_DIM
    share = latent_n // tile_n
    few = tile_n == 4
    part_n = 4
    part_rows = latent_n // part_n
    place = lax.axis_index("tiles") if few else jnp.int32(0)
    place = place.astype(jnp.int32).reshape(1)
    others = (part_n - 1) * part_rows
    main = pl.pallas_call(
        lambda *refs: main_kernel(part_n, *refs),
        name="main",
        out_shape=(
            jax.ShapeDtypeStruct((others, width), F32),
            jax.ShapeDtypeStruct((others, width), F32),
            jax.ShapeDtypeStruct((4 * tokens, width), BF16),
            jax.ShapeDtypeStruct((4 * tokens, width), BF16),
            jax.ShapeDtypeStruct((8, 4 * tokens), F32),
        ),
        in_specs=[smem_spec()] + [vmem_spec()] * 7,
        out_specs=(vmem_spec(),) * 5,
        compiler_params=pltpu.CompilerParams(vmem_limit_bytes=16 * MIB),
        cost_estimate=pl.CostEstimate(flops=10**6, bytes_accessed=10**4, transcendentals=0),
    )(place, message, near, far, far_near, w_key, w_value, queries)
    rest = pl.pallas_call(
        lambda *refs: rest_kernel(part_n, *refs),
        name="rest",
        out_shape=(
            jax.ShapeDtypeStruct((8 * quarter, width), BF16),
            jax.ShapeDtypeStruct((8 * quarter, width), BF16),
            jax.ShapeDtypeStruct((8, 8 * quarter), F32),
        ) + (jax.ShapeDtypeStruct((part_rows + 8, width), F32),) * (part_n - 1),
        in_specs=[smem_spec()] + [vmem_spec()] * 9,
        out_specs=(vmem_spec(),) * (part_n + 2),
        compiler_params=pltpu.CompilerParams(vmem_limit_bytes=12 * MIB),
        cost_estimate=pl.CostEstimate(
            flops=20 * 10**9, bytes_accessed=4 * 10**7, transcendentals=0
        ),
    )(place, rim, *rims, w_key, w_value, queries, main[0], main[1])
    own = pl.pallas_call(
        lambda *refs: own_kernel(part_n, *refs),
        name="own",
        out_shape=jax.ShapeDtypeStruct((part_rows + 8, width), F32),
        in_specs=[smem_spec()] + [vmem_spec()] * 7,
        out_specs=vmem_spec(),
        compiler_params=pltpu.CompilerParams(vmem_limit_bytes=12 * MIB),
        cost_estimate=pl.CostEstimate(flops=10**9, bytes_accessed=4 * 10**6, transcendentals=0),
    )(place, queries, main[2], main[3], main[4], rest[0], rest[1], rest[2])
    parts = (own,) + tuple(rest[3:])

    if few:
        received = [swapped(parts[k], "tiles", k) for k in (1, 2, 3)]
        return pl.pallas_call(
            lambda *refs: merge_kernel(head_n, *refs),
            name="merge",
            out_shape=jax.ShapeDtypeStruct((part_rows, width), BF16),
            in_specs=[vmem_spec()] * 4,
            out_specs=vmem_spec(),
            compiler_params=pltpu.CompilerParams(vmem_limit_bytes=4 * MIB),
        )(parts[0], *received)
    parts = jnp.stack(parts)
    stats = parts[:, part_rows : part_rows + 4]
    stats = stats.transpose(0, 2, 1).reshape(tile_n, share, 4)
    weighted = parts[:, :part_rows].reshape(tile_n, share, width)
    stats = lax.all_to_all(stats, "tiles", 0, 0)
    weighted = lax.all_to_all(weighted, "tiles", 0, 0)
    peaks, totals = stats[..., :head_n], stats[..., head_n : 2 * head_n]
    scale = jnp.exp(peaks - jnp.max(peaks, axis=0, keepdims=True))
    scale = scale / jnp.sum(scale * totals, axis=0, keepdims=True)
    return jnp.sum(weighted * jnp.repeat(scale, HEAD_DIM, axis=2), axis=0).astype(BF16)


def solution(mesh):
    in_specs = (
        P(("slides", "tiles", "heads"), None, None),
        P(),
        P(),
        P(),
        P(None, "heads"),
        P(None, "heads"),
        P(None, "heads"),
        P(("slides", "tiles", "heads")),
        P(("slides", "tiles", "heads")),
        P(("slides", "tiles", "heads"), None),
    )
    out_specs = P(("slides", "tiles"), "heads")
    return jax.shard_map(
        per_device, mesh=mesh, in_specs=in_specs, out_specs=out_specs, check_vma=False
    )
```

```python
import jax
import jax.numpy as jnp
from jax import lax
from jax.experimental import pallas as pl
from jax.experimental.pallas import tpu as pltpu
from jax.sharding import PartitionSpec as P

HEAD_DIM = 64
NEG_BIG = -1e30
LN_EPS = 1e-05
F32 = jnp.float32
BF16 = jnp.bfloat16
VMEM = pltpu.VMEM
SMEM = pltpu.SMEM
MIB = 1 << 20
FIRST_VMEM = 20 * MIB
ORDER = (3, 0, 2, 1)


def vmem_spec():
    return pl.BlockSpec(memory_space=VMEM)


def smem_spec():
    return pl.BlockSpec(memory_space=SMEM)


def wide_dots(cells, dense_ref):
    part, out_n = dense_ref.shape[0] // 4, dense_ref.shape[1] // 4
    return [
        jnp.dot(
            cells[:, first * part : last * part],
            dense_ref[pl.ds(first * part, (last - first) * part), pl.ds(b * out_n, out_n)],
            preferred_element_type=F32,
        )
        for b, (first, last) in enumerate(((0, 4), (0, 2), (1, 3), (1, 2)))
    ]


def expand_weights(flat, in_group, out_group, dense_ref, order=(0, 1, 2, 3)):
    groups = flat.shape[0] // (9 * in_group)
    wide = groups * out_group
    source = lax.broadcasted_iota(jnp.int32, (out_group, wide), 0)
    target = lax.broadcasted_iota(jnp.int32, (out_group, wide), 1)
    spread = (lax.rem(target, out_group) == source).astype(BF16)
    tiled = jnp.dot(flat, spread, preferred_element_type=F32)
    row = lax.broadcasted_iota(jnp.int32, tiled.shape, 0)
    lane = lax.broadcasted_iota(jnp.int32, tiled.shape, 1)
    own = lax.div(row, 9 * in_group) == lax.div(lane, out_group)
    tiled = jnp.where(own, tiled, 0.0).astype(BF16)
    dense_ref[...] = jnp.zeros_like(dense_ref)
    for group in range(groups):
        for tap_row in range(3):
            for tap_col in range(3):
                py, px = int(tap_row != 1), int(tap_col != 1)
                block = 2 * int(tap_row == 0) + int(tap_col == 0)
                first = (9 * group + 3 * tap_row + tap_col) * in_group
                to_row = order[2 * py + px] * groups * in_group + group * in_group
                dense_ref[pl.ds(to_row, in_group), pl.ds(block * wide, wide)] = tiled[
                    first : first + in_group
                ]


def shifted_down(x):
    row = lax.broadcasted_iota(jnp.int32, x.shape, 0)
    return jnp.where(row == 0, 0.0, pltpu.roll(x, 1, 0))


def normalised(deep):
    deep = jnp.maximum(deep, 0.0)
    centred = deep - jnp.mean(deep, axis=1, keepdims=True)
    spread = jnp.mean(centred * centred, axis=1, keepdims=True)
    return (centred * lax.rsqrt(spread + LN_EPS)).astype(BF16)


def expand_kernel(w1_ref, w2_ref, dense1_ref, dense2_ref):
    expand_weights(w1_ref[...], w1_ref.shape[0] // 36, w1_ref.shape[1], dense1_ref)
    expand_weights(w2_ref[...], w2_ref.shape[0] // 36, w2_ref.shape[1], dense2_ref, ORDER)


def opening_kernel(out_ref):
    out_ref[...] = jnp.zeros_like(out_ref)


def counts_kernel(count_ref, tissue_ref, opened_ref, out_ref):
    live = (count_ref[0] > 0).astype(F32)
    row = lax.broadcasted_iota(jnp.int32, out_ref.shape, 0)
    out_ref[...] = jnp.where(row == 0, live, live * tissue_ref[0].astype(F32))


def first_kernel(side, counts_ref, adjacency_ref, weight, w1, w2, pixels, token_ref,
                 edge_ref, border_ref, tiny_ref, cells_ref, even_lines, odd_lines, dense1_ref,
                 dense2_ref, wide1, partial, cells, wide2):
    expand_weights(w1[...], w1.shape[0] // 36, w1.shape[1], dense1_ref)
    expand_weights(w2[...], w2.shape[0] // 36, w2.shape[1], dense2_ref, ORDER)
    stem_n, half = weight.shape[0], side // 2
    rows, span = 4 * half, 4 * side
    row = lax.broadcasted_iota(jnp.int32, (rows, 2 * span), 0)
    column = lax.broadcasted_iota(jnp.int32, (rows, 2 * span), 1)
    line = 2 * lax.div(lax.rem(row, 2 * half), half) + lax.div(row, 2 * half)
    wanted = line * side + 2 * lax.rem(row, half)
    pick = (lax.rem(column, span) == wanted + lax.div(column, span)).astype(BF16)
    live, known = counts_ref[pl.ds(0, 1), pl.ds(0, 1)], counts_ref[pl.ds(1, 1), pl.ds(0, 1)]
    gates = [(adjacency_ref[:, k : k + 1] == 0).astype(F32) for k in range(3)]
    row = lax.broadcasted_iota(jnp.int32, (16, cells_ref.shape[1]), 0)
    facts = jnp.zeros(row.shape, F32)
    for k, fact in enumerate([live] + gates + [known]):
        facts = jnp.where(row == k, fact, facts)
    cells_ref[pl.ds(half * half, 16)] = facts.astype(BF16)
    border_ref[pl.ds(4 * half, 16)] = facts.astype(BF16)
    flat = jnp.dot(weight[...], pixels[0], preferred_element_type=F32)
    flat = (jnp.maximum(flat, 0.0) * live).astype(BF16)
    blank = jnp.zeros((stem_n, span), BF16)
    for k in range(side // 4):
        four = flat[:, k * span : (k + 1) * span]
        both = jnp.concatenate(
            [jnp.concatenate([four, blank], axis=0), jnp.concatenate([blank, four], axis=0)],
            axis=1,
        )
        sorted_ = lax.dot_general(
            pick, both, (((1,), (1,)), ((), ())), preferred_element_type=F32
        )
        here = pl.ds(k * 2 * half, 2 * half)
        even_lines[here] = sorted_[: 2 * half]
        odd_lines[here] = sorted_[2 * half :]
        cells_ref[here, pl.ds(0, 2 * stem_n)] = sorted_[: 2 * half].astype(BF16)
        cells_ref[here, pl.ds(2 * stem_n, 2 * stem_n)] = sorted_[2 * half :].astype(BF16)
    border_ref[pl.ds(0, 2 * half)] = cells_ref[pl.ds((half - 2) * half, 2 * half)]
    for which in range(2):
        for py, lines in enumerate((even_lines, odd_lines)):
            border_ref[
                pl.ds((2 + which) * half, half), pl.ds(py * 2 * stem_n, 2 * stem_n)
            ] = lines[pl.ds(half - 2 + which, half, stride=half)].astype(BF16)
    tiny_ref[pl.ds(0, 16)] = cells_ref[pl.ds((half - 1) * half - 16, 16)]
    tiny_ref[pl.ds(16, 16)] = cells_ref[pl.ds(half * half - 16, 16)]
    positions, channels = partial.shape
    chunk = 8 * half
    wide1[pl.ds(0, half)] = jnp.zeros((half, wide1.shape[1]), F32)
    row = lax.broadcasted_iota(jnp.int32, (chunk, channels), 0)
    first = lax.rem(row, half) == 0
    dense = dense1_ref[...]
    lane = [pl.ds(b * channels, channels) for b in range(4)]
    for k in range(positions // chunk):
        wide1[pl.ds(half + k * chunk, chunk)] = jnp.dot(
            cells_ref[pl.ds(k * chunk, chunk)], dense, preferred_element_type=F32
        )
        here = pl.ds(half + k * chunk, chunk)
        up = pl.ds(k * chunk, chunk)
        before = wide1[here, lane[1]] + wide1[up, lane[3]]
        before = jnp.where(first, 0.0, pltpu.roll(before, 1, 0))
        partial[pl.ds(k * chunk, chunk)] = wide1[here, lane[0]] + wide1[up, lane[2]] + before
    edge_ref[pl.ds(0, 2 * half)] = partial[pl.ds(0, 2 * half)]
    edge_ref[pl.ds(2 * half, half)] = partial[pl.ds(0, half, stride=half)]
    edge_ref[pl.ds(3 * half, half)] = partial[pl.ds(1, half, stride=half)]
    edge_ref[pl.ds(4 * half, 8)] = facts[0:8, :channels]
    quarter = half // 2
    for i in range(half):
        for px in range(2):
            cells[
                pl.ds((i // 2) * quarter, quarter),
                pl.ds(ORDER[2 * (i % 2) + px] * channels, channels),
            ] = jnp.maximum(partial[pl.ds(i * half + px, quarter, stride=2)], 0.0).astype(BF16)
    tokens = quarter * quarter
    out_n = dense2_ref.shape[1] // 4
    block = [pl.ds(b * out_n, out_n) for b in range(4)]
    wide2[pl.ds(0, quarter)] = jnp.zeros((quarter, wide2.shape[1]), F32)
    here, up = pl.ds(quarter, tokens), pl.ds(0, tokens)
    for b, product in enumerate(wide_dots(cells[...], dense2_ref)):
        wide2[here, block[b]] = product
    before = wide2[here, block[1]] + wide2[up, block[3]]
    row = lax.broadcasted_iota(jnp.int32, before.shape, 0)
    before = jnp.where(lax.rem(row, quarter) == 0, 0.0, pltpu.roll(before, 1, 0))
    deep = wide2[here, block[0]] + wide2[up, block[2]] + before
    token_ref[pl.ds(0, tokens)] = normalised(deep)
    token_ref[pl.ds(tokens, 16)] = cells_ref[pl.ds(positions, 16)]


def rim_kernel(edge_ref, prior_ref, second_ref, dense1_ref, dense2_ref, rim_ref,
               lines, cells):
    half, channels = (edge_ref.shape[0] - 8) // 4, edge_ref.shape[1]
    quarter = half // 2
    facts = edge_ref[pl.ds(4 * half, 8)]
    live, above, beside, corner, known = [facts[k : k + 1, 0:1] for k in range(5)]
    lane = [slice(b * channels, (b + 1) * channels) for b in range(4)]
    dense1 = dense1_ref[...]
    prior = jnp.dot(prior_ref[pl.ds(0, 4 * half)], dense1, preferred_element_type=F32)
    second = jnp.dot(second_ref[...], dense1, preferred_element_type=F32)
    facts = prior_ref[pl.ds(4 * half, 16), pl.ds(0, channels)].astype(F32)
    live_prior, above_prior, beside_prior = facts[0:1], facts[1:2], facts[2:3]
    row_30 = prior[0:half]
    row_31 = prior[half : 2 * half]
    col_30 = prior[2 * half : 3 * half]
    col_31 = prior[3 * half : 4 * half]
    at_zero = lax.broadcasted_iota(jnp.int32, (half, channels), 0) == 0
    top = above * (row_31[:, lane[2]] + shifted_down(row_31[:, lane[3]]))
    top = top + jnp.where(at_zero, corner * row_31[half - 1 : half, lane[3]], 0.0)
    side = beside * (col_31[:, lane[1]] + shifted_down(col_31[:, lane[3]]))
    own = [edge_ref[pl.ds(k * half, half)] for k in range(4)]
    own[0] = own[0] + top + jnp.where(at_zero, side, 0.0)
    own[1] = own[1] + jnp.where(at_zero, side[1:2], 0.0)
    own[2] = own[2] + side + jnp.where(at_zero, top, 0.0)
    own[3] = own[3] + jnp.where(at_zero, top[1:2], 0.0)
    for k in range(4):
        lines[pl.ds(k * half, half)] = jnp.maximum(own[k], 0.0) * live
    over_last, left_last, last = second[15:16], second[30:31], second[31:32]
    row_sum = row_31[:, lane[0]] + row_30[:, lane[2]]
    row_sum = row_sum + shifted_down(row_31[:, lane[1]] + row_30[:, lane[3]])
    row_sum = row_sum + jnp.where(
        at_zero, beside_prior * (last[:, lane[1]] + over_last[:, lane[3]]), 0.0
    )
    col_sum = col_31[:, lane[0]] + col_30[:, lane[1]]
    col_sum = col_sum + shifted_down(col_31[:, lane[2]] + col_30[:, lane[3]])
    col_sum = col_sum + jnp.where(
        at_zero, above_prior * (last[:, lane[2]] + left_last[:, lane[3]]), 0.0
    )
    lines[pl.ds(4 * half, half)] = jnp.maximum(row_sum, 0.0) * live_prior
    lines[pl.ds(5 * half, half)] = jnp.maximum(col_sum, 0.0) * live_prior
    cells[pl.ds(2 * quarter, 2 * quarter)] = jnp.zeros((2 * quarter, cells.shape[1]), BF16)

    def put(which, py, px, line, parity):
        cells[pl.ds(which * quarter, quarter), pl.ds(ORDER[2 * py + px] * channels, channels)] = lines[
            pl.ds(line * half + parity, quarter, stride=2)
        ].astype(BF16)

    for a in range(2):
        for b in range(2):
            put(0, a, b, a, b)
            put(1, a, b, 2 + b, a)
        put(2, 1, a, 4, a)
        put(3, a, 1, 5, a)
    out_n = dense2_ref.shape[1] // 4
    wide = wide_dots(cells[...], dense2_ref)
    part = [[wide[b][k * quarter : (k + 1) * quarter] for b in range(4)] for k in range(4)]
    row0, col0, over, left = part
    at_zero = lax.broadcasted_iota(jnp.int32, (quarter, out_n), 0) == 0
    deep_row = row0[0] + shifted_down(row0[1]) + above * (over[2] + shifted_down(over[3]))
    deep_row = deep_row + jnp.where(
        at_zero, beside * left[1] + corner * over[3][quarter - 1 : quarter], 0.0
    )
    deep_col = col0[0] + shifted_down(col0[2]) + beside * (left[1] + shifted_down(left[3]))
    rim_ref[pl.ds(0, quarter)] = normalised(deep_row)
    rim_ref[pl.ds(quarter, quarter)] = normalised(deep_col)
    rim_ref[pl.ds(2 * quarter, 16)] = jnp.broadcast_to(known, (16, out_n)).astype(BF16)


def queries_of(place_ref, q_ref, parts, part_n):
    rows = q_ref.shape[0] // part_n
    found = [
        q_ref[pl.ds(pl.multiple_of((place_ref[0] ^ k) * rows, rows), rows)].astype(F32)
        for k in parts
    ]
    return jnp.concatenate(found, axis=0) * (float(HEAD_DIM) ** -0.5)


def by_head(q):
    lane = lax.broadcasted_iota(jnp.int32, q.shape, 1)
    head_n = q.shape[1] // HEAD_DIM
    return jnp.concatenate(
        [jnp.where(lax.div(lane, HEAD_DIM) == h, q, 0.0) for h in range(head_n)], axis=0
    ).astype(BF16)


def softmax_part(q, pieces):
    rows, width = q.shape
    head_n = width // HEAD_DIM
    lane = lax.broadcasted_iota(jnp.int32, (rows, width), 1)
    q = by_head(q)
    scores = [
        lax.dot_general(q, keys, (((1,), (1,)), ((), ())), preferred_element_type=F32) + bias
        for keys, _, bias in pieces
    ]
    peak = jnp.max(scores[0], axis=1, keepdims=True)
    for more in scores[1:]:
        peak = jnp.maximum(peak, jnp.max(more, axis=1, keepdims=True))
    total = summed = 0.0
    for score, (_, values, _) in zip(scores, pieces):
        weights = jnp.exp(score - peak)
        total = total + jnp.sum(weights, axis=1, keepdims=True)
        summed = summed + jnp.dot(weights.astype(BF16), values, preferred_element_type=F32)
    joined = summed[:rows]
    facts = jnp.zeros((rows, width), F32)
    for h in range(head_n):
        mine = slice(h * rows, (h + 1) * rows)
        joined = jnp.where(lax.div(lane, HEAD_DIM) == h, summed[mine], joined)
        facts = jnp.where(lane == h, peak[mine], facts)
        facts = jnp.where(lane == head_n + h, total[mine], facts)
    return joined, facts


def main_kernel(part_n, place_ref, t0, t1, t2, t3, wk_ref, wv_ref, q_ref, sum_ref, facts_ref,
                keys, values, bias_ref):
    tokens = t0.shape[0] - 16
    quarter = int(round(tokens**0.5))
    width = q_ref.shape[1]
    both = jnp.concatenate([wk_ref[...], wv_ref[...]], axis=1)
    masks = []
    spot = lax.broadcasted_iota(jnp.int32, (1, tokens), 1)
    inside = (spot >= quarter) & (lax.rem(spot, quarter) != 0)
    for b, ref in enumerate((t0, t1, t2, t3)):
        made = jnp.dot(ref[pl.ds(0, tokens)], both, preferred_element_type=F32).astype(BF16)
        keys[pl.ds(b * tokens, tokens)] = made[:, :width]
        values[pl.ds(b * tokens, tokens)] = made[:, width:]
        known = ref[pl.ds(tokens, 16), pl.ds(0, tokens)].astype(F32)[4:5]
        masks.append(jnp.where(inside & (spot.astype(F32) < known), 0.0, NEG_BIG))
    bias = jnp.concatenate(masks, axis=1)
    bias_ref[...] = jnp.broadcast_to(bias, bias_ref.shape)
    rows = sum_ref.shape[0] // (part_n - 1)
    pieces = [(keys[...], values[...], bias)]
    for k in range(1, part_n):
        here = pl.ds((k - 1) * rows, rows)
        q = queries_of(place_ref, q_ref, [k], part_n)
        sum_ref[here], facts_ref[here] = softmax_part(q, pieces)


def rest_kernel(part_n, place_ref, t0, t1, t2, t3, wk_ref, wv_ref, q_ref, sum_ref, before_ref,
                keys, values, bias_ref, *out_refs):
    rim = t0.shape[0] - 16
    quarter = rim // 2
    width = q_ref.shape[1]
    head_n = width // HEAD_DIM
    both = jnp.concatenate([wk_ref[...], wv_ref[...]], axis=1)
    spot = lax.broadcasted_iota(jnp.int32, (1, rim), 1)
    token = jnp.where(spot < quarter, spot, (spot - quarter) * quarter)
    masks = []
    for ref in (t0, t1, t2, t3):
        known = ref[pl.ds(rim, 16), pl.ds(0, rim)].astype(F32)[0:1]
        good = (spot != quarter) & (token.astype(F32) < known)
        masks.append(jnp.where(good, 0.0, NEG_BIG))
    bias = jnp.concatenate(masks, axis=1)
    bias_ref[...] = jnp.broadcast_to(bias, bias_ref.shape)
    all_rim = jnp.concatenate([ref[pl.ds(0, rim)] for ref in (t0, t1, t2, t3)], axis=0)
    made = jnp.dot(all_rim, both, preferred_element_type=F32).astype(BF16)
    keys[...] = made[:, :width]
    values[...] = made[:, width:]
    q = queries_of(place_ref, q_ref, range(1, part_n), part_n)
    joined, facts = softmax_part(q, [(made[:, :width], made[:, width:], bias)])
    lane = lax.broadcasted_iota(jnp.int32, facts.shape, 1)
    before = before_ref[...]
    peak = jnp.maximum(facts, before)
    scale_new = jnp.exp(jnp.where(lane < head_n, facts - peak, 0.0))
    scale_old = jnp.exp(jnp.where(lane < head_n, before - peak, 0.0))
    total = facts * pltpu.roll(scale_new, head_n, 1) + before * pltpu.roll(scale_old, head_n, 1)
    wide_new, wide_old = scale_new[:, 0:1], scale_old[:, 0:1]
    for h in range(1, head_n):
        mine = lax.div(lane, HEAD_DIM) == h
        wide_new = jnp.where(mine, scale_new[:, h : h + 1], wide_new)
        wide_old = jnp.where(mine, scale_old[:, h : h + 1], wide_old)
    joined = joined * wide_new + sum_ref[...] * wide_old
    facts = jnp.where(lane < head_n, peak, total)
    rows = q_ref.shape[0] // part_n
    for k, out_ref in enumerate(out_refs):
        out_ref[pl.ds(0, rows)] = joined[k * rows : (k + 1) * rows]
        out_ref[pl.ds(rows, 8)] = facts[k * rows : (k + 1) * rows].T[0:8]


def own_kernel(part_n, place_ref, q_ref, keys, values, bias_ref, rim_keys, rim_values,
               rim_bias_ref, out_ref):
    joined, facts = softmax_part(
        queries_of(place_ref, q_ref, [0], part_n),
        [
            (keys[...], values[...], bias_ref[pl.ds(0, 1)]),
            (rim_keys[...], rim_values[...], rim_bias_ref[pl.ds(0, 1)]),
        ],
    )
    rows = q_ref.shape[0] // part_n
    out_ref[pl.ds(0, rows)] = joined
    out_ref[pl.ds(rows, 8)] = facts.T[0:8]


def merge_kernel(head_n, *refs):
    in_refs, out_ref = refs[:-1], refs[-1]
    part_rows, width = out_ref.shape
    stats = [ref[pl.ds(part_rows, 8)] for ref in in_refs]
    row8 = lax.broadcasted_iota(jnp.int32, stats[0].shape, 0)
    peak = stats[0]
    for s in stats[1:]:
        peak = jnp.maximum(peak, s)
    scales = [jnp.exp(jnp.where(row8 < head_n, s - peak, 0.0)) for s in stats]
    total = scales[0] * pltpu.roll(stats[0], 8 - head_n, 0)
    for c, s in zip(scales[1:], stats[1:]):
        total = total + c * pltpu.roll(s, 8 - head_n, 0)
    total = jnp.where(row8 < head_n, total, 1.0)
    scales = [c / total for c in scales]
    blank = jnp.zeros((part_rows - 8 * len(scales), part_rows), F32)
    turned = jnp.concatenate(scales + [blank], axis=0).T
    lane = lax.broadcasted_iota(jnp.int32, (part_rows, width), 1)
    result = jnp.zeros((part_rows, width), F32)
    for k, ref in enumerate(in_refs):
        scale = turned[:, 8 * k : 8 * k + 1]
        for h in range(1, head_n):
            scale = jnp.where(
                lax.div(lane, HEAD_DIM) == h, turned[:, 8 * k + h : 8 * k + h + 1], scale
            )
        result = result + ref[pl.ds(0, part_rows)] * scale
    out_ref[...] = result.astype(BF16)


def swapped(x, axis, distance):
    return lax.ppermute(x, axis, [(i, i ^ distance) for i in range(lax.axis_size(axis))])


def per_device(
    pixels, w_stem, w_conv1, w_conv2, w_key, w_value, queries, tile_count, tissue, adjacency
):
    slot_n, area, patch = pixels.shape
    assert slot_n == 1
    side = int(round(area**0.5))
    half, quarter = side // 2, side // 4
    channels = w_stem.shape[1]
    groups, _, in1, out1 = w_conv1.shape
    _, _, in2, out2 = w_conv2.shape
    mid_n, out_n = groups * out1, groups * out2
    tokens = quarter * quarter
    border_rows = 4 * half + 16

    w1 = w_conv1.reshape(groups * 9 * in1, out1)
    w2 = w_conv2.reshape(groups * 9 * in2, out2)
    dense_shapes = ((4 * channels, 4 * mid_n), (4 * mid_n, 4 * out_n))
    opened = pl.pallas_call(
        opening_kernel,
        name="opening",
        out_shape=jax.ShapeDtypeStruct((8, 128), F32),
        out_specs=vmem_spec(),
        compiler_params=pltpu.CompilerParams(vmem_limit_bytes=1 * MIB),
        cost_estimate=pl.CostEstimate(
            flops=20 * 10**9, bytes_accessed=4 * 10**7, transcendentals=0
        ),
    )()
    opened, tile_count, tissue = lax.optimization_barrier((opened, tile_count, tissue))
    counts = pl.pallas_call(
        counts_kernel,
        name="counts",
        out_shape=jax.ShapeDtypeStruct((8, 128), F32),
        in_specs=[smem_spec()] * 2 + [vmem_spec()],
        out_specs=vmem_spec(),
        compiler_params=pltpu.CompilerParams(vmem_limit_bytes=1 * MIB),
    )(tile_count, tissue, opened)
    message, edge, border, tiny = pl.pallas_call(
        lambda *refs: first_kernel(side, *refs),
        name="first",
        out_shape=(
            jax.ShapeDtypeStruct((tokens + 16, out_n), BF16),
            jax.ShapeDtypeStruct((4 * half + 8, mid_n), F32),
            jax.ShapeDtypeStruct((border_rows, 4 * channels), BF16),
            jax.ShapeDtypeStruct((32, 4 * channels), BF16),
        ),
        in_specs=[vmem_spec()] * 6,
        out_specs=(vmem_spec(),) * 4,
        scratch_shapes=[
            VMEM((half * half + 16, 4 * channels), BF16),
            VMEM((half * half, 2 * channels), F32),
            VMEM((half * half, 2 * channels), F32),
            VMEM(dense_shapes[0], BF16),
            VMEM(dense_shapes[1], BF16),
            VMEM((half * half + half, 4 * mid_n), F32),
            VMEM((half * half, mid_n), F32),
            VMEM((tokens, 4 * mid_n), BF16),
            VMEM((tokens + quarter, 4 * out_n), F32),
        ],
        compiler_params=pltpu.CompilerParams(vmem_limit_bytes=FIRST_VMEM),
    )(
        counts, adjacency, w_stem.T, w1, w2,
        jnp.swapaxes(pixels, 1, 2),
    )

    line = ("tiles", "heads")
    line_n = lax.axis_size("tiles") * lax.axis_size("heads")
    prior = lax.ppermute(border, line, [(i, i + 1) for i in range(line_n - 1)])
    second = lax.ppermute(tiny, line, [(i, i + 2) for i in range(line_n - 2)])
    message, w1, w2 = lax.optimization_barrier((message, w1, w2))
    dense1, dense2 = pl.pallas_call(
        expand_kernel,
        name="expand",
        out_shape=tuple(jax.ShapeDtypeStruct(shape, BF16) for shape in dense_shapes),
        in_specs=[vmem_spec()] * 2,
        out_specs=(vmem_spec(),) * 2,
        compiler_params=pltpu.CompilerParams(vmem_limit_bytes=8 * MIB),
        cost_estimate=pl.CostEstimate(flops=10**9, bytes_accessed=4 * 10**6, transcendentals=0),
    )(w1, w2)
    far = swapped(message, "heads", 2)
    message_n, dense1, prior = lax.optimization_barrier((message, dense1, prior))
    near = swapped(message_n, "heads", 1)
    far_near = swapped(far, "heads", 1)

    rim = pl.pallas_call(
        rim_kernel,
        name="rim",
        out_shape=jax.ShapeDtypeStruct((2 * quarter + 16, out_n), BF16),
        in_specs=[vmem_spec()] * 5,
        out_specs=vmem_spec(),
        scratch_shapes=[
            VMEM((6 * half, mid_n), F32),
            VMEM((4 * quarter, 4 * mid_n), BF16),
        ],
        compiler_params=pltpu.CompilerParams(vmem_limit_bytes=12 * MIB),
        cost_estimate=pl.CostEstimate(flops=20*10**9, bytes_accessed=4 * 10**7, transcendentals=0),
    )(edge, prior, second, dense1, dense2)
    rims = [swapped(rim, "heads", k) for k in (2, 1, 3)]

    tile_n = lax.axis_size("tiles")
    latent_n, width = queries.shape
    head_n = width // HEAD_DIM
    share = latent_n // tile_n
    few = tile_n == 4
    part_n = 4
    part_rows = latent_n // part_n
    place = lax.axis_index("tiles") if few else jnp.int32(0)
    place = place.astype(jnp.int32).reshape(1)
    others = (part_n - 1) * part_rows
    main = pl.pallas_call(
        lambda *refs: main_kernel(part_n, *refs),
        name="main",
        out_shape=(
            jax.ShapeDtypeStruct((others, width), F32),
            jax.ShapeDtypeStruct((others, width), F32),
            jax.ShapeDtypeStruct((4 * tokens, width), BF16),
            jax.ShapeDtypeStruct((4 * tokens, width), BF16),
            jax.ShapeDtypeStruct((8, 4 * tokens), F32),
        ),
        in_specs=[smem_spec()] + [vmem_spec()] * 7,
        out_specs=(vmem_spec(),) * 5,
        compiler_params=pltpu.CompilerParams(vmem_limit_bytes=16 * MIB),
        cost_estimate=pl.CostEstimate(flops=10**6, bytes_accessed=10**4, transcendentals=0),
    )(place, message, near, far, far_near, w_key, w_value, queries)
    rest = pl.pallas_call(
        lambda *refs: rest_kernel(part_n, *refs),
        name="rest",
        out_shape=(
            jax.ShapeDtypeStruct((8 * quarter, width), BF16),
            jax.ShapeDtypeStruct((8 * quarter, width), BF16),
            jax.ShapeDtypeStruct((8, 8 * quarter), F32),
        ) + (jax.ShapeDtypeStruct((part_rows + 8, width), F32),) * (part_n - 1),
        in_specs=[smem_spec()] + [vmem_spec()] * 9,
        out_specs=(vmem_spec(),) * (part_n + 2),
        compiler_params=pltpu.CompilerParams(vmem_limit_bytes=12 * MIB),
        cost_estimate=pl.CostEstimate(
            flops=20 * 10**9, bytes_accessed=4 * 10**7, transcendentals=0
        ),
    )(place, rim, *rims, w_key, w_value, queries, main[0], main[1])
    own = pl.pallas_call(
        lambda *refs: own_kernel(part_n, *refs),
        name="own",
        out_shape=jax.ShapeDtypeStruct((part_rows + 8, width), F32),
        in_specs=[smem_spec()] + [vmem_spec()] * 7,
        out_specs=vmem_spec(),
        compiler_params=pltpu.CompilerParams(vmem_limit_bytes=12 * MIB),
        cost_estimate=pl.CostEstimate(flops=10**9, bytes_accessed=4 * 10**6, transcendentals=0),
    )(place, queries, main[2], main[3], main[4], rest[0], rest[1], rest[2])
    parts = (own,) + tuple(rest[3:])

    if few:
        received = [swapped(parts[k], "tiles", k) for k in (1, 2, 3)]
        return pl.pallas_call(
            lambda *refs: merge_kernel(head_n, *refs),
            name="merge",
            out_shape=jax.ShapeDtypeStruct((part_rows, width), BF16),
            in_specs=[vmem_spec()] * 4,
            out_specs=vmem_spec(),
            compiler_params=pltpu.CompilerParams(vmem_limit_bytes=4 * MIB),
        )(parts[0], *received)
    parts = jnp.stack(parts)
    stats = parts[:, part_rows : part_rows + 4]
    stats = stats.transpose(0, 2, 1).reshape(tile_n, share, 4)
    weighted = parts[:, :part_rows].reshape(tile_n, share, width)
    stats = lax.all_to_all(stats, "tiles", 0, 0)
    weighted = lax.all_to_all(weighted, "tiles", 0, 0)
    peaks, totals = stats[..., :head_n], stats[..., head_n : 2 * head_n]
    scale = jnp.exp(peaks - jnp.max(peaks, axis=0, keepdims=True))
    scale = scale / jnp.sum(scale * totals, axis=0, keepdims=True)
    return jnp.sum(weighted * jnp.repeat(scale, HEAD_DIM, axis=2), axis=0).astype(BF16)


def solution(mesh):
    in_specs = (
        P(("slides", "tiles", "heads"), None, None),
        P(),
        P(),
        P(),
        P(None, "heads"),
        P(None, "heads"),
        P(None, "heads"),
        P(("slides", "tiles", "heads")),
        P(("slides", "tiles", "heads")),
        P(("slides", "tiles", "heads"), None),
    )
    out_specs = P(("slides", "tiles"), "heads")
    return jax.shard_map(
        per_device, mesh=mesh, in_specs=in_specs, out_specs=out_specs, check_vma=False
    )
```

```python
import jax
import jax.numpy as jnp
from jax import lax
from jax.experimental import pallas as pl
from jax.experimental.pallas import tpu as pltpu
from jax.sharding import PartitionSpec as P

HEAD_DIM = 64
NEG_BIG = -1e30
LN_EPS = 1e-05
F32 = jnp.float32
BF16 = jnp.bfloat16
VMEM = pltpu.VMEM
SMEM = pltpu.SMEM
MIB = 1 << 20
FIRST_VMEM = 20 * MIB
ORDER = (3, 0, 2, 1)


def vmem_spec():
    return pl.BlockSpec(memory_space=VMEM)


def smem_spec():
    return pl.BlockSpec(memory_space=SMEM)


def wide_dots(cells, dense_ref):
    part, out_n = dense_ref.shape[0] // 4, dense_ref.shape[1] // 4
    return [
        jnp.dot(
            cells[:, first * part : last * part],
            dense_ref[pl.ds(first * part, (last - first) * part), pl.ds(b * out_n, out_n)],
            preferred_element_type=F32,
        )
        for b, (first, last) in enumerate(((0, 4), (0, 2), (1, 3), (1, 2)))
    ]


def expand_weights(flat, in_group, out_group, dense_ref, order=(0, 1, 2, 3)):
    groups = flat.shape[0] // (9 * in_group)
    wide = groups * out_group
    source = lax.broadcasted_iota(jnp.int32, (out_group, wide), 0)
    target = lax.broadcasted_iota(jnp.int32, (out_group, wide), 1)
    spread = (lax.rem(target, out_group) == source).astype(BF16)
    tiled = jnp.dot(flat, spread, preferred_element_type=F32)
    row = lax.broadcasted_iota(jnp.int32, tiled.shape, 0)
    lane = lax.broadcasted_iota(jnp.int32, tiled.shape, 1)
    own = lax.div(row, 9 * in_group) == lax.div(lane, out_group)
    tiled = jnp.where(own, tiled, 0.0).astype(BF16)
    dense_ref[...] = jnp.zeros_like(dense_ref)
    for group in range(groups):
        for tap_row in range(3):
            for tap_col in range(3):
                py, px = int(tap_row != 1), int(tap_col != 1)
                block = 2 * int(tap_row == 0) + int(tap_col == 0)
                first = (9 * group + 3 * tap_row + tap_col) * in_group
                to_row = order[2 * py + px] * groups * in_group + group * in_group
                dense_ref[pl.ds(to_row, in_group), pl.ds(block * wide, wide)] = tiled[
                    first : first + in_group
                ]


def shifted_down(x):
    row = lax.broadcasted_iota(jnp.int32, x.shape, 0)
    return jnp.where(row == 0, 0.0, pltpu.roll(x, 1, 0))


def normalised(deep):
    deep = jnp.maximum(deep, 0.0)
    centred = deep - jnp.mean(deep, axis=1, keepdims=True)
    spread = jnp.mean(centred * centred, axis=1, keepdims=True)
    return (centred * lax.rsqrt(spread + LN_EPS)).astype(BF16)


def opening_kernel(out_ref):
    out_ref[...] = jnp.zeros_like(out_ref)


def counts_kernel(count_ref, tissue_ref, opened_ref, out_ref):
    live = (count_ref[0] > 0).astype(F32)
    row = lax.broadcasted_iota(jnp.int32, out_ref.shape, 0)
    out_ref[...] = jnp.where(row == 0, live, live * tissue_ref[0].astype(F32))


def first_kernel(side, counts_ref, adjacency_ref, weight, w1, w2, pixels, token_ref,
                 edge_ref, border_ref, tiny_ref, dense1_ref, dense2_ref, cells_ref, even_lines,
                 odd_lines, wide1, partial, cells, wide2):
    expand_weights(w1[...], w1.shape[0] // 36, w1.shape[1], dense1_ref)
    expand_weights(w2[...], w2.shape[0] // 36, w2.shape[1], dense2_ref, ORDER)
    stem_n, half = weight.shape[0], side // 2
    rows, span = 4 * half, 4 * side
    row = lax.broadcasted_iota(jnp.int32, (rows, 2 * span), 0)
    column = lax.broadcasted_iota(jnp.int32, (rows, 2 * span), 1)
    line = 2 * lax.div(lax.rem(row, 2 * half), half) + lax.div(row, 2 * half)
    wanted = line * side + 2 * lax.rem(row, half)
    pick = (lax.rem(column, span) == wanted + lax.div(column, span)).astype(BF16)
    live, known = counts_ref[pl.ds(0, 1), pl.ds(0, 1)], counts_ref[pl.ds(1, 1), pl.ds(0, 1)]
    gates = [(adjacency_ref[:, k : k + 1] == 0).astype(F32) for k in range(3)]
    row = lax.broadcasted_iota(jnp.int32, (16, cells_ref.shape[1]), 0)
    facts = jnp.zeros(row.shape, F32)
    for k, fact in enumerate([live] + gates + [known]):
        facts = jnp.where(row == k, fact, facts)
    cells_ref[pl.ds(half * half, 16)] = facts.astype(BF16)
    border_ref[pl.ds(4 * half, 16)] = facts.astype(BF16)
    flat = jnp.dot(weight[...], pixels[0], preferred_element_type=F32)
    flat = (jnp.maximum(flat, 0.0) * live).astype(BF16)
    blank = jnp.zeros((stem_n, span), BF16)
    for k in range(side // 4):
        four = flat[:, k * span : (k + 1) * span]
        both = jnp.concatenate(
            [jnp.concatenate([four, blank], axis=0), jnp.concatenate([blank, four], axis=0)],
            axis=1,
        )
        sorted_ = lax.dot_general(
            pick, both, (((1,), (1,)), ((), ())), preferred_element_type=F32
        )
        here = pl.ds(k * 2 * half, 2 * half)
        even_lines[here] = sorted_[: 2 * half]
        odd_lines[here] = sorted_[2 * half :]
        cells_ref[here, pl.ds(0, 2 * stem_n)] = sorted_[: 2 * half].astype(BF16)
        cells_ref[here, pl.ds(2 * stem_n, 2 * stem_n)] = sorted_[2 * half :].astype(BF16)
    border_ref[pl.ds(0, 2 * half)] = cells_ref[pl.ds((half - 2) * half, 2 * half)]
    for which in range(2):
        for py, lines in enumerate((even_lines, odd_lines)):
            border_ref[
                pl.ds((2 + which) * half, half), pl.ds(py * 2 * stem_n, 2 * stem_n)
            ] = lines[pl.ds(half - 2 + which, half, stride=half)].astype(BF16)
    tiny_ref[pl.ds(0, 16)] = cells_ref[pl.ds((half - 1) * half - 16, 16)]
    tiny_ref[pl.ds(16, 16)] = cells_ref[pl.ds(half * half - 16, 16)]
    positions, channels = partial.shape
    chunk = 4 * half
    wide1[pl.ds(0, half)] = jnp.zeros((half, wide1.shape[1]), F32)
    row = lax.broadcasted_iota(jnp.int32, (chunk, channels), 0)
    first = lax.rem(row, half) == 0
    dense = dense1_ref[...]
    lane = [pl.ds(b * channels, channels) for b in range(4)]
    for k in range(positions // chunk):
        wide1[pl.ds(half + k * chunk, chunk)] = jnp.dot(
            cells_ref[pl.ds(k * chunk, chunk)], dense, preferred_element_type=F32
        )
        here = pl.ds(half + k * chunk, chunk)
        up = pl.ds(k * chunk, chunk)
        before = wide1[here, lane[1]] + wide1[up, lane[3]]
        before = jnp.where(first, 0.0, pltpu.roll(before, 1, 0))
        partial[pl.ds(k * chunk, chunk)] = wide1[here, lane[0]] + wide1[up, lane[2]] + before
    edge_ref[pl.ds(0, 2 * half)] = partial[pl.ds(0, 2 * half)]
    edge_ref[pl.ds(2 * half, half)] = partial[pl.ds(0, half, stride=half)]
    edge_ref[pl.ds(3 * half, half)] = partial[pl.ds(1, half, stride=half)]
    edge_ref[pl.ds(4 * half, 8)] = facts[0:8, :channels]
    quarter = half // 2
    for i in range(half):
        for px in range(2):
            cells[
                pl.ds((i // 2) * quarter, quarter),
                pl.ds(ORDER[2 * (i % 2) + px] * channels, channels),
            ] = jnp.maximum(partial[pl.ds(i * half + px, quarter, stride=2)], 0.0).astype(BF16)
    tokens = quarter * quarter
    out_n = dense2_ref.shape[1] // 4
    block = [pl.ds(b * out_n, out_n) for b in range(4)]
    wide2[pl.ds(0, quarter)] = jnp.zeros((quarter, wide2.shape[1]), F32)
    here, up = pl.ds(quarter, tokens), pl.ds(0, tokens)
    for b, product in enumerate(wide_dots(cells[...], dense2_ref)):
        wide2[here, block[b]] = product
    before = wide2[here, block[1]] + wide2[up, block[3]]
    row = lax.broadcasted_iota(jnp.int32, before.shape, 0)
    before = jnp.where(lax.rem(row, quarter) == 0, 0.0, pltpu.roll(before, 1, 0))
    deep = wide2[here, block[0]] + wide2[up, block[2]] + before
    token_ref[pl.ds(0, tokens)] = normalised(deep)
    token_ref[pl.ds(tokens, 16)] = cells_ref[pl.ds(positions, 16)]


def rim_kernel(edge_ref, prior_ref, second_ref, dense1_ref, dense2_ref, rim_ref,
               lines, cells):
    half, channels = (edge_ref.shape[0] - 8) // 4, edge_ref.shape[1]
    quarter = half // 2
    facts = edge_ref[pl.ds(4 * half, 8)]
    live, above, beside, corner, known = [facts[k : k + 1, 0:1] for k in range(5)]
    lane = [slice(b * channels, (b + 1) * channels) for b in range(4)]
    dense1 = dense1_ref[...]
    prior = jnp.dot(prior_ref[pl.ds(0, 4 * half)], dense1, preferred_element_type=F32)
    second = jnp.dot(second_ref[...], dense1, preferred_element_type=F32)
    facts = prior_ref[pl.ds(4 * half, 16), pl.ds(0, channels)].astype(F32)
    live_prior, above_prior, beside_prior = facts[0:1], facts[1:2], facts[2:3]
    row_30 = prior[0:half]
    row_31 = prior[half : 2 * half]
    col_30 = prior[2 * half : 3 * half]
    col_31 = prior[3 * half : 4 * half]
    at_zero = lax.broadcasted_iota(jnp.int32, (half, channels), 0) == 0
    top = above * (row_31[:, lane[2]] + shifted_down(row_31[:, lane[3]]))
    top = top + jnp.where(at_zero, corner * row_31[half - 1 : half, lane[3]], 0.0)
    side = beside * (col_31[:, lane[1]] + shifted_down(col_31[:, lane[3]]))
    own = [edge_ref[pl.ds(k * half, half)] for k in range(4)]
    own[0] = own[0] + top + jnp.where(at_zero, side, 0.0)
    own[1] = own[1] + jnp.where(at_zero, side[1:2], 0.0)
    own[2] = own[2] + side + jnp.where(at_zero, top, 0.0)
    own[3] = own[3] + jnp.where(at_zero, top[1:2], 0.0)
    for k in range(4):
        lines[pl.ds(k * half, half)] = jnp.maximum(own[k], 0.0) * live
    over_last, left_last, last = second[15:16], second[30:31], second[31:32]
    row_sum = row_31[:, lane[0]] + row_30[:, lane[2]]
    row_sum = row_sum + shifted_down(row_31[:, lane[1]] + row_30[:, lane[3]])
    row_sum = row_sum + jnp.where(
        at_zero, beside_prior * (last[:, lane[1]] + over_last[:, lane[3]]), 0.0
    )
    col_sum = col_31[:, lane[0]] + col_30[:, lane[1]]
    col_sum = col_sum + shifted_down(col_31[:, lane[2]] + col_30[:, lane[3]])
    col_sum = col_sum + jnp.where(
        at_zero, above_prior * (last[:, lane[2]] + left_last[:, lane[3]]), 0.0
    )
    lines[pl.ds(4 * half, half)] = jnp.maximum(row_sum, 0.0) * live_prior
    lines[pl.ds(5 * half, half)] = jnp.maximum(col_sum, 0.0) * live_prior
    cells[pl.ds(2 * quarter, 2 * quarter)] = jnp.zeros((2 * quarter, cells.shape[1]), BF16)

    def put(which, py, px, line, parity):
        cells[pl.ds(which * quarter, quarter), pl.ds(ORDER[2 * py + px] * channels, channels)] = lines[
            pl.ds(line * half + parity, quarter, stride=2)
        ].astype(BF16)

    for a in range(2):
        for b in range(2):
            put(0, a, b, a, b)
            put(1, a, b, 2 + b, a)
        put(2, 1, a, 4, a)
        put(3, a, 1, 5, a)
    out_n = dense2_ref.shape[1] // 4
    wide = wide_dots(cells[...], dense2_ref)
    part = [[wide[b][k * quarter : (k + 1) * quarter] for b in range(4)] for k in range(4)]
    row0, col0, over, left = part
    at_zero = lax.broadcasted_iota(jnp.int32, (quarter, out_n), 0) == 0
    deep_row = row0[0] + shifted_down(row0[1]) + above * (over[2] + shifted_down(over[3]))
    deep_row = deep_row + jnp.where(
        at_zero, beside * left[1] + corner * over[3][quarter - 1 : quarter], 0.0
    )
    deep_col = col0[0] + shifted_down(col0[2]) + beside * (left[1] + shifted_down(left[3]))
    rim_ref[pl.ds(0, quarter)] = normalised(deep_row)
    rim_ref[pl.ds(quarter, quarter)] = normalised(deep_col)
    rim_ref[pl.ds(2 * quarter, 16)] = jnp.broadcast_to(known, (16, out_n)).astype(BF16)


def queries_of(place_ref, q_ref, parts, part_n):
    rows = q_ref.shape[0] // part_n
    found = [
        q_ref[pl.ds(pl.multiple_of((place_ref[0] ^ k) * rows, rows), rows)].astype(F32)
        for k in parts
    ]
    return jnp.concatenate(found, axis=0) * (float(HEAD_DIM) ** -0.5)


def by_head(q):
    lane = lax.broadcasted_iota(jnp.int32, q.shape, 1)
    head_n = q.shape[1] // HEAD_DIM
    return jnp.concatenate(
        [jnp.where(lax.div(lane, HEAD_DIM) == h, q, 0.0) for h in range(head_n)], axis=0
    ).astype(BF16)


def softmax_part(q, pieces):
    rows, width = q.shape
    head_n = width // HEAD_DIM
    lane = lax.broadcasted_iota(jnp.int32, (rows, width), 1)
    q = by_head(q)
    scores = [
        lax.dot_general(q, keys, (((1,), (1,)), ((), ())), preferred_element_type=F32) + bias
        for keys, _, bias in pieces
    ]
    peak = jnp.max(scores[0], axis=1, keepdims=True)
    for more in scores[1:]:
        peak = jnp.maximum(peak, jnp.max(more, axis=1, keepdims=True))
    total = summed = 0.0
    for score, (_, values, _) in zip(scores, pieces):
        weights = jnp.exp(score - peak)
        total = total + jnp.sum(weights, axis=1, keepdims=True)
        summed = summed + jnp.dot(weights.astype(BF16), values, preferred_element_type=F32)
    joined = summed[:rows]
    facts = jnp.zeros((rows, width), F32)
    for h in range(head_n):
        mine = slice(h * rows, (h + 1) * rows)
        joined = jnp.where(lax.div(lane, HEAD_DIM) == h, summed[mine], joined)
        facts = jnp.where(lane == h, peak[mine], facts)
        facts = jnp.where(lane == head_n + h, total[mine], facts)
    return joined, facts


def main_kernel(part_n, place_ref, t0, t1, t2, t3, wk_ref, wv_ref, q_ref, sum_ref, facts_ref,
                keys, values, bias_ref):
    tokens = t0.shape[0] - 16
    quarter = int(round(tokens**0.5))
    width = q_ref.shape[1]
    both = jnp.concatenate([wk_ref[...], wv_ref[...]], axis=1)
    masks = []
    spot = lax.broadcasted_iota(jnp.int32, (1, tokens), 1)
    inside = (spot >= quarter) & (lax.rem(spot, quarter) != 0)
    for b, ref in enumerate((t0, t1, t2, t3)):
        made = jnp.dot(ref[pl.ds(0, tokens)], both, preferred_element_type=F32).astype(BF16)
        keys[pl.ds(b * tokens, tokens)] = made[:, :width]
        values[pl.ds(b * tokens, tokens)] = made[:, width:]
        known = ref[pl.ds(tokens, 16), pl.ds(0, tokens)].astype(F32)[4:5]
        masks.append(jnp.where(inside & (spot.astype(F32) < known), 0.0, NEG_BIG))
    bias = jnp.concatenate(masks, axis=1)
    bias_ref[...] = jnp.broadcast_to(bias, bias_ref.shape)
    rows = sum_ref.shape[0] // (part_n - 1)
    pieces = [(keys[...], values[...], bias)]
    for k in range(1, part_n):
        here = pl.ds((k - 1) * rows, rows)
        q = queries_of(place_ref, q_ref, [k], part_n)
        sum_ref[here], facts_ref[here] = softmax_part(q, pieces)


def rest_kernel(part_n, place_ref, t0, t1, t2, t3, wk_ref, wv_ref, q_ref, sum_ref, before_ref,
                keys, values, bias_ref, *out_refs):
    rim = t0.shape[0] - 16
    quarter = rim // 2
    width = q_ref.shape[1]
    head_n = width // HEAD_DIM
    both = jnp.concatenate([wk_ref[...], wv_ref[...]], axis=1)
    spot = lax.broadcasted_iota(jnp.int32, (1, rim), 1)
    token = jnp.where(spot < quarter, spot, (spot - quarter) * quarter)
    masks = []
    for ref in (t0, t1, t2, t3):
        known = ref[pl.ds(rim, 16), pl.ds(0, rim)].astype(F32)[0:1]
        good = (spot != quarter) & (token.astype(F32) < known)
        masks.append(jnp.where(good, 0.0, NEG_BIG))
    bias = jnp.concatenate(masks, axis=1)
    bias_ref[...] = jnp.broadcast_to(bias, bias_ref.shape)
    all_rim = jnp.concatenate([ref[pl.ds(0, rim)] for ref in (t0, t1, t2, t3)], axis=0)
    made = jnp.dot(all_rim, both, preferred_element_type=F32).astype(BF16)
    keys[...] = made[:, :width]
    values[...] = made[:, width:]
    q = queries_of(place_ref, q_ref, range(1, part_n), part_n)
    joined, facts = softmax_part(q, [(made[:, :width], made[:, width:], bias)])
    lane = lax.broadcasted_iota(jnp.int32, facts.shape, 1)
    before = before_ref[...]
    peak = jnp.maximum(facts, before)
    scale_new = jnp.exp(jnp.where(lane < head_n, facts - peak, 0.0))
    scale_old = jnp.exp(jnp.where(lane < head_n, before - peak, 0.0))
    total = facts * pltpu.roll(scale_new, head_n, 1) + before * pltpu.roll(scale_old, head_n, 1)
    wide_new, wide_old = scale_new[:, 0:1], scale_old[:, 0:1]
    for h in range(1, head_n):
        mine = lax.div(lane, HEAD_DIM) == h
        wide_new = jnp.where(mine, scale_new[:, h : h + 1], wide_new)
        wide_old = jnp.where(mine, scale_old[:, h : h + 1], wide_old)
    joined = joined * wide_new + sum_ref[...] * wide_old
    facts = jnp.where(lane < head_n, peak, total)
    rows = q_ref.shape[0] // part_n
    for k, out_ref in enumerate(out_refs):
        out_ref[pl.ds(0, rows)] = joined[k * rows : (k + 1) * rows]
        out_ref[pl.ds(rows, 8)] = facts[k * rows : (k + 1) * rows].T[0:8]


def own_kernel(part_n, place_ref, q_ref, keys, values, bias_ref, rim_keys, rim_values,
               rim_bias_ref, out_ref):
    joined, facts = softmax_part(
        queries_of(place_ref, q_ref, [0], part_n),
        [
            (keys[...], values[...], bias_ref[pl.ds(0, 1)]),
            (rim_keys[...], rim_values[...], rim_bias_ref[pl.ds(0, 1)]),
        ],
    )
    rows = q_ref.shape[0] // part_n
    out_ref[pl.ds(0, rows)] = joined
    out_ref[pl.ds(rows, 8)] = facts.T[0:8]


def merge_kernel(head_n, *refs):
    in_refs, out_ref = refs[:-1], refs[-1]
    part_rows, width = out_ref.shape
    stats = [ref[pl.ds(part_rows, 8)] for ref in in_refs]
    row8 = lax.broadcasted_iota(jnp.int32, stats[0].shape, 0)
    peak = stats[0]
    for s in stats[1:]:
        peak = jnp.maximum(peak, s)
    scales = [jnp.exp(jnp.where(row8 < head_n, s - peak, 0.0)) for s in stats]
    total = scales[0] * pltpu.roll(stats[0], 8 - head_n, 0)
    for c, s in zip(scales[1:], stats[1:]):
        total = total + c * pltpu.roll(s, 8 - head_n, 0)
    total = jnp.where(row8 < head_n, total, 1.0)
    scales = [c / total for c in scales]
    blank = jnp.zeros((part_rows - 8 * len(scales), part_rows), F32)
    turned = jnp.concatenate(scales + [blank], axis=0).T
    lane = lax.broadcasted_iota(jnp.int32, (part_rows, width), 1)
    result = jnp.zeros((part_rows, width), F32)
    for k, ref in enumerate(in_refs):
        scale = turned[:, 8 * k : 8 * k + 1]
        for h in range(1, head_n):
            scale = jnp.where(
                lax.div(lane, HEAD_DIM) == h, turned[:, 8 * k + h : 8 * k + h + 1], scale
            )
        result = result + ref[pl.ds(0, part_rows)] * scale
    out_ref[...] = result.astype(BF16)


def swapped(x, axis, distance):
    return lax.ppermute(x, axis, [(i, i ^ distance) for i in range(lax.axis_size(axis))])


def per_device(
    pixels, w_stem, w_conv1, w_conv2, w_key, w_value, queries, tile_count, tissue, adjacency
):
    slot_n, area, patch = pixels.shape
    assert slot_n == 1
    side = int(round(area**0.5))
    half, quarter = side // 2, side // 4
    channels = w_stem.shape[1]
    groups, _, in1, out1 = w_conv1.shape
    _, _, in2, out2 = w_conv2.shape
    mid_n, out_n = groups * out1, groups * out2
    tokens = quarter * quarter
    border_rows = 4 * half + 16

    w1 = w_conv1.reshape(groups * 9 * in1, out1)
    w2 = w_conv2.reshape(groups * 9 * in2, out2)
    dense_shapes = ((4 * channels, 4 * mid_n), (4 * mid_n, 4 * out_n))
    opened = pl.pallas_call(
        opening_kernel,
        name="opening",
        out_shape=jax.ShapeDtypeStruct((8, 128), F32),
        out_specs=vmem_spec(),
        compiler_params=pltpu.CompilerParams(vmem_limit_bytes=1 * MIB),
        cost_estimate=pl.CostEstimate(
            flops=20 * 10**9, bytes_accessed=4 * 10**7, transcendentals=0
        ),
    )()
    opened, tile_count, tissue = lax.optimization_barrier((opened, tile_count, tissue))
    counts = pl.pallas_call(
        counts_kernel,
        name="counts",
        out_shape=jax.ShapeDtypeStruct((8, 128), F32),
        in_specs=[smem_spec()] * 2 + [vmem_spec()],
        out_specs=vmem_spec(),
        compiler_params=pltpu.CompilerParams(vmem_limit_bytes=1 * MIB),
    )(tile_count, tissue, opened)
    message, edge, border, tiny, dense1, dense2 = pl.pallas_call(
        lambda *refs: first_kernel(side, *refs),
        name="first",
        out_shape=(
            jax.ShapeDtypeStruct((tokens + 16, out_n), BF16),
            jax.ShapeDtypeStruct((4 * half + 8, mid_n), F32),
            jax.ShapeDtypeStruct((border_rows, 4 * channels), BF16),
            jax.ShapeDtypeStruct((32, 4 * channels), BF16),
        ) + tuple(jax.ShapeDtypeStruct(shape, BF16) for shape in dense_shapes),
        in_specs=[vmem_spec()] * 6,
        out_specs=(vmem_spec(),) * 6,
        scratch_shapes=[
            VMEM((half * half + 16, 4 * channels), BF16),
            VMEM((half * half, 2 * channels), F32),
            VMEM((half * half, 2 * channels), F32),
            VMEM((half * half + half, 4 * mid_n), F32),
            VMEM((half * half, mid_n), F32),
            VMEM((tokens, 4 * mid_n), BF16),
            VMEM((tokens + quarter, 4 * out_n), F32),
        ],
        compiler_params=pltpu.CompilerParams(vmem_limit_bytes=FIRST_VMEM),
    )(
        counts, adjacency, w_stem.T, w1, w2,
        jnp.swapaxes(pixels, 1, 2),
    )

    line = ("tiles", "heads")
    line_n = lax.axis_size("tiles") * lax.axis_size("heads")
    prior = lax.ppermute(border, line, [(i, i + 1) for i in range(line_n - 1)])
    second = lax.ppermute(tiny, line, [(i, i + 2) for i in range(line_n - 2)])
    far = swapped(message, "heads", 2)
    message_n, prior = lax.optimization_barrier((message, prior))
    near = swapped(message_n, "heads", 1)
    far_near = swapped(far, "heads", 1)

    rim = pl.pallas_call(
        rim_kernel,
        name="rim",
        out_shape=jax.ShapeDtypeStruct((2 * quarter + 16, out_n), BF16),
        in_specs=[vmem_spec()] * 5,
        out_specs=vmem_spec(),
        scratch_shapes=[
            VMEM((6 * half, mid_n), F32),
            VMEM((4 * quarter, 4 * mid_n), BF16),
        ],
        compiler_params=pltpu.CompilerParams(vmem_limit_bytes=12 * MIB),
        cost_estimate=pl.CostEstimate(flops=20*10**9, bytes_accessed=4 * 10**7, transcendentals=0),
    )(edge, prior, second, dense1, dense2)
    rims = [swapped(rim, "heads", k) for k in (2, 1, 3)]

    tile_n = lax.axis_size("tiles")
    latent_n, width = queries.shape
    head_n = width // HEAD_DIM
    share = latent_n // tile_n
    few = tile_n == 4
    part_n = 4
    part_rows = latent_n // part_n
    place = lax.axis_index("tiles") if few else jnp.int32(0)
    place = place.astype(jnp.int32).reshape(1)
    others = (part_n - 1) * part_rows
    main = pl.pallas_call(
        lambda *refs: main_kernel(part_n, *refs),
        name="main",
        out_shape=(
            jax.ShapeDtypeStruct((others, width), F32),
            jax.ShapeDtypeStruct((others, width), F32),
            jax.ShapeDtypeStruct((4 * tokens, width), BF16),
            jax.ShapeDtypeStruct((4 * tokens, width), BF16),
            jax.ShapeDtypeStruct((8, 4 * tokens), F32),
        ),
        in_specs=[smem_spec()] + [vmem_spec()] * 7,
        out_specs=(vmem_spec(),) * 5,
        compiler_params=pltpu.CompilerParams(vmem_limit_bytes=16 * MIB),
        cost_estimate=pl.CostEstimate(flops=10**6, bytes_accessed=10**4, transcendentals=0),
    )(place, message, near, far, far_near, w_key, w_value, queries)
    rest = pl.pallas_call(
        lambda *refs: rest_kernel(part_n, *refs),
        name="rest",
        out_shape=(
            jax.ShapeDtypeStruct((8 * quarter, width), BF16),
            jax.ShapeDtypeStruct((8 * quarter, width), BF16),
            jax.ShapeDtypeStruct((8, 8 * quarter), F32),
        ) + (jax.ShapeDtypeStruct((part_rows + 8, width), F32),) * (part_n - 1),
        in_specs=[smem_spec()] + [vmem_spec()] * 9,
        out_specs=(vmem_spec(),) * (part_n + 2),
        compiler_params=pltpu.CompilerParams(vmem_limit_bytes=12 * MIB),
        cost_estimate=pl.CostEstimate(
            flops=20 * 10**9, bytes_accessed=4 * 10**7, transcendentals=0
        ),
    )(place, rim, *rims, w_key, w_value, queries, main[0], main[1])
    own = pl.pallas_call(
        lambda *refs: own_kernel(part_n, *refs),
        name="own",
        out_shape=jax.ShapeDtypeStruct((part_rows + 8, width), F32),
        in_specs=[smem_spec()] + [vmem_spec()] * 7,
        out_specs=vmem_spec(),
        compiler_params=pltpu.CompilerParams(vmem_limit_bytes=12 * MIB),
        cost_estimate=pl.CostEstimate(flops=10**9, bytes_accessed=4 * 10**6, transcendentals=0),
    )(place, queries, main[2], main[3], main[4], rest[0], rest[1], rest[2])
    parts = (own,) + tuple(rest[3:])

    if few:
        received = [swapped(parts[k], "tiles", k) for k in (3, 2, 1)]
        return pl.pallas_call(
            lambda *refs: merge_kernel(head_n, *refs),
            name="merge",
            out_shape=jax.ShapeDtypeStruct((part_rows, width), BF16),
            in_specs=[vmem_spec()] * 4,
            out_specs=vmem_spec(),
            compiler_params=pltpu.CompilerParams(vmem_limit_bytes=4 * MIB),
        )(parts[0], *received)
    parts = jnp.stack(parts)
    stats = parts[:, part_rows : part_rows + 4]
    stats = stats.transpose(0, 2, 1).reshape(tile_n, share, 4)
    weighted = parts[:, :part_rows].reshape(tile_n, share, width)
    stats = lax.all_to_all(stats, "tiles", 0, 0)
    weighted = lax.all_to_all(weighted, "tiles", 0, 0)
    peaks, totals = stats[..., :head_n], stats[..., head_n : 2 * head_n]
    scale = jnp.exp(peaks - jnp.max(peaks, axis=0, keepdims=True))
    scale = scale / jnp.sum(scale * totals, axis=0, keepdims=True)
    return jnp.sum(weighted * jnp.repeat(scale, HEAD_DIM, axis=2), axis=0).astype(BF16)


def solution(mesh):
    in_specs = (
        P(("slides", "tiles", "heads"), None, None),
        P(),
        P(),
        P(),
        P(None, "heads"),
        P(None, "heads"),
        P(None, "heads"),
        P(("slides", "tiles", "heads")),
        P(("slides", "tiles", "heads")),
        P(("slides", "tiles", "heads"), None),
    )
    out_specs = P(("slides", "tiles"), "heads")
    return jax.shard_map(
        per_device, mesh=mesh, in_specs=in_specs, out_specs=out_specs, check_vma=False
    )
```
